512 devices in a mesh: stack: 16 (over y, core), flow: 8 (over z), width: 4 (over x).
Axes of the slice: x: 4, y: 8, z: 8, core: 2. Of those that a mesh axis runs over, the one named last changes fastest.
Arguments:
- initial_thermal_state: float32 [256, 1024, 1024], P('stack', 'flow', 'width'), may hold values from -6 to 6
- plate_fluid_category: int32 [256], replicated, may hold values from 0 to 2
- corrugation_type_grid: int32 [256, 1024], P('stack', 'flow'), may hold values from 0 to 3
Outputs:
- new_temperature: float32 [256, 1024, 1024], P('stack', 'flow', 'width')
The draws below stay inside these ranges and needn't reach their ends.
Inputs may be any that keep to these rules, and one draw needn't show every extreme that they name: `plate_fluid_category`: 0 is a hot stream layer, 1 a cold stream layer, 2 a parting sheet. `corrugation_type_grid`: selects a column of the conductivity and film tables.
All inputs are finite; a program needn't handle non-finite values.
Results may differ from the reference program's by a relative error of at most 0.0003.
Values sent between devices are 32-bit elements; how exact they have to be, the bound alone decides.
A program may use at most 64 MiB of HBM per device.

```python
import jax
import jax.numpy as jnp
from jax import lax

PLATE_TOTAL = 256
STREAMWISE_LINES = 1024
SPANWISE_LINES = 1024


def with_ends(drawn, rng, least, high):
    place = [jax.random.randint(jax.random.fold_in(rng, axis), (), 0, length) for axis, length in enumerate(drawn.shape)]
    main_axis = drawn.shape.index(max(drawn.shape))
    beside = place[:main_axis] + [(place[main_axis] + 1) % drawn.shape[main_axis]] + place[main_axis + 1:]
    return drawn.at[tuple(place)].set(least).at[tuple(beside)].set(high)


def steps_of(own_key, extent, cuts, smallest, top_value):
    def one(axis_at, shards_of):
        heights = jax.random.uniform(jax.random.fold_in(jax.random.fold_in(own_key, 6), axis_at), (shards_of,), jnp.float32, smallest / len(cuts), top_value / len(cuts))
        return jnp.repeat(jnp.exp(heights), extent[axis_at] // shards_of).reshape((-1,) + (1,) * (len(extent) - axis_at - 1))

    loudness = one(*cuts[0])
    for cut in cuts[1:]:
        loudness = loudness * one(*cut)
    return loudness


def noise(rng, dims, width, most, pieces=(), kind=jnp.bfloat16):
    entries = jax.random.normal(rng, dims, jnp.float32) * width
    if len(pieces) > 0:
        entries = steps_of(rng, dims, pieces, -0.22, 0.18) * entries
    return jnp.clip(entries, min=-most, max=most).astype(kind)


def setup_inputs(seed: int = 0) -> dict:
    seeds = jax.random.split(jax.random.key(seed), 4)
    initial_thermal_state = noise(seeds[0], (PLATE_TOTAL, STREAMWISE_LINES, SPANWISE_LINES), 1.0, 6.0, ((0, 16), (1, 8), (2, 4)), jnp.float32)
    plate_fluid_category = with_ends(jax.random.randint(seeds[1], (PLATE_TOTAL,), 0, 3), jax.random.fold_in(seeds[1], 1), 0, 2).astype(jnp.int32)
    corrugation_type_grid = with_ends(jax.random.randint(seeds[2], (PLATE_TOTAL, STREAMWISE_LINES), 0, 4), jax.random.fold_in(seeds[2], 1), 0, 3).astype(jnp.int32)
    return {"initial_thermal_state": initial_thermal_state, "plate_fluid_category": plate_fluid_category, "corrugation_type_grid": corrugation_type_grid}


stack_conductance = (0.15, 0.25, 1.0)
plane_conductance = ((0.35, 0.5, 0.7, 0.9), (0.3, 0.45, 0.65, 0.85), (0.8, 0.9, 1.0, 0.95))
film_coefficient = ((0.4, 0.8, 1.2, 1.6), (0.3, 0.6, 1.0, 1.4), (0.0, 0.0, 0.0, 0.0))
stream_level = (1.5, -1.0, 0.0)
inplane_update = 0.24
stack_scale = 0.2


def face_weight(centre, beside):
    return 2.0 * centre * beside / (centre + beside)


def inplane_flux(padded_t, padded_k, centre_t, centre_k):
    accumulated = face_weight(centre_k, padded_k[..., 2:, 1:-1]) * (padded_t[..., 2:, 1:-1] - centre_t)
    accumulated = accumulated + face_weight(centre_k, padded_k[..., :-2, 1:-1]) * (padded_t[..., :-2, 1:-1] - centre_t)
    accumulated = accumulated + face_weight(centre_k, padded_k[..., 1:-1, 2:]) * (padded_t[..., 1:-1, 2:] - centre_t)
    accumulated = accumulated + face_weight(centre_k, padded_k[..., 1:-1, :-2]) * (padded_t[..., 1:-1, :-2] - centre_t)
    return accumulated


def broaden(plane_part, template):
    return plane_part.reshape(plane_part.shape + (1,) * (template.ndim - plane_part.ndim))


def thomas_solve(below_link, diagonal, above_link, rhs_list):
    def forward(state_now, row_data):
        ratio_prev, partial_prev = state_now
        link_low, middle, link_high, rights = row_data
        pivot_value = middle - link_low * ratio_prev
        ratio_now = link_high / pivot_value
        partial_now = tuple((item + broaden(link_low, item) * prior) / broaden(pivot_value, item)
                            for item, prior in zip(rights, partial_prev))
        return (ratio_now, partial_now), (ratio_now, partial_now)

    start_state = (jnp.zeros_like(diagonal[0]), tuple(jnp.zeros_like(item[0]) for item in rhs_list))
    _, (ratios, partials) = lax.scan(forward, start_state, (below_link, diagonal, above_link, tuple(rhs_list)))

    def backward(following, row_data):
        ratio_now, partial_now = row_data
        values = tuple(part + broaden(ratio_now, part) * later for part, later in zip(partial_now, following))
        return values, values

    start_values = tuple(jnp.zeros_like(item[0]) for item in rhs_list)
    _, solved = lax.scan(backward, start_values, (ratios, partials), reverse=True)
    return solved


def reference(initial_thermal_state, plate_fluid_category, corrugation_type_grid):
    stack_k = jnp.asarray(stack_conductance, jnp.float32)[plate_fluid_category]
    coupling = stack_scale * float(PLATE_TOTAL * PLATE_TOTAL) * face_weight(stack_k[:-1], stack_k[1:])
    upper_link = jnp.concatenate([coupling, jnp.zeros((1,), jnp.float32)])
    lower_link = jnp.concatenate([jnp.zeros((1,), jnp.float32), coupling])
    lateral_transmission = jnp.asarray(plane_conductance, jnp.float32)[plate_fluid_category[:, None], corrugation_type_grid]
    surface_coefficient_map = jnp.asarray(film_coefficient, jnp.float32)[plate_fluid_category[:, None], corrugation_type_grid]
    tier_collected = jnp.asarray(stream_level, jnp.float32)[plate_fluid_category]

    def plate_forcing_vector(row_data):
        temp_layer, k_layer, film_layer, level_layer = row_data
        k_wide = jnp.broadcast_to(k_layer[:, None], temp_layer.shape)
        stack_heat_flux = inplane_flux(jnp.pad(temp_layer, 1), jnp.pad(k_wide, 1), temp_layer, k_wide)
        return temp_layer + inplane_update * stack_heat_flux + (film_layer * level_layer)[:, None]

    linear_system_target = lax.map(plate_forcing_vector, (initial_thermal_state, lateral_transmission, surface_coefficient_map, tier_collected))
    diagonal = 1.0 + surface_coefficient_map + lower_link[:, None] + upper_link[:, None]
    below_wide = jnp.broadcast_to(lower_link[:, None], diagonal.shape)
    above_wide = jnp.broadcast_to(upper_link[:, None], diagonal.shape)
    solved = thomas_solve(below_wide, diagonal, above_wide, (linear_system_target,))
    return solved[0]
```

```python
import functools

import jax
import jax.numpy as jnp
from jax import lax
from jax.experimental import pallas as pl
from jax.experimental.pallas import tpu as pltpu
from jax.sharding import PartitionSpec as P

STACK_K = (0.15, 0.25, 1.0)
PLANE_K = ((0.35, 0.5, 0.7, 0.9), (0.3, 0.45, 0.65, 0.85), (0.8, 0.9, 1.0, 0.95))
FILM = ((0.4, 0.8, 1.2, 1.6), (0.3, 0.6, 1.0, 1.4), (0.0, 0.0, 0.0, 0.0))
LEVEL = (1.5, -1.0, 0.0)
INPLANE = 0.24
STACK_SCALE = 0.2
MESH = pl.DeviceIdType.MESH
SUB = 8
LANES = 128


def face(a, b):
    return 2.0 * a * b / (a + b)


def pick_scalar(code, values):
    out = jnp.float32(values[-1])
    for i in range(len(values) - 2, -1, -1):
        out = jnp.where(code == i, jnp.float32(values[i]), out)
    return out


def pick_pair(index, table):
    flat = [v for row in table for v in row]
    out = jnp.full(index.shape, flat[-1], jnp.float32)
    for i in range(len(flat) - 2, -1, -1):
        if flat[i] != flat[-1]:
            out = jnp.where(index == i, jnp.float32(flat[i]), out)
    return out


def link(scale, first, second):
    rows = []
    for a in STACK_K:
        rows.append(pick_scalar(second, [scale * face(a, b) for b in STACK_K]))
    return jnp.where(first == 0, rows[0], jnp.where(first == 1, rows[1], rows[2]))


def lane(tile, q, width):
    return jnp.broadcast_to(tile[:, q : q + 1], (tile.shape[0], width))


def kernel(
    dims,
    cat_ref,
    corr_ref,
    t_hbm,
    out_ref,
    tbuf,
    e_own,
    e_left,
    e_right,
    corr_dn,
    corr_up,
    cbuf,
    ct,
    ct_rx,
    ld_tx,
    ld_rx,
    sol_tx,
    sol_rx,
    piv,
    t_sem,
    halo_send,
    halo_recv,
    ct_send,
    ct_recv,
    ld_send,
    ld_recv,
    sol_send,
    sol_recv,
):
    ns, nf, nw, nl, nr, nc, scale = dims
    tiles = nr // SUB
    me, fi, wi = lax.axis_index("stack"), lax.axis_index("flow"), lax.axis_index("width")
    f_next, f_prev = lax.rem(fi + 1, nf), lax.rem(fi + nf - 1, nf)
    w_next, w_prev = lax.rem(wi + 1, nw), lax.rem(wi + nw - 1, nw)
    base = me * nl
    half = ns // 2

    load = pltpu.make_async_copy(t_hbm, tbuf.at[:, pl.ds(SUB, nr), :], t_sem)
    load.start()

    barrier = pltpu.get_barrier_semaphore()
    for dev in ({"flow": f_next}, {"flow": f_prev}, {"width": w_next}, {"width": w_prev}):
        pl.semaphore_signal(barrier, inc=1, device_id=dev, device_id_type=MESH)

    @pl.loop(1, ns)
    def _(i):
        pl.semaphore_signal(
            barrier, inc=1, device_id={"stack": lax.rem(me + i, ns)}, device_id_type=MESH
        )

    pl.semaphore_wait(barrier, ns - 1 + 4)

    def remote(src, dst, k, dev):
        return pltpu.make_async_remote_copy(
            src_ref=src,
            dst_ref=dst,
            send_sem=halo_send.at[k],
            recv_sem=halo_recv.at[k],
            device_id=dev,
            device_id_type=MESH,
        )

    row_dn = remote(t_hbm.at[:, pl.ds(nr - SUB, SUB), :], tbuf.at[:, pl.ds(0, SUB), :], 0, {"flow": f_next})
    row_up = remote(t_hbm.at[:, pl.ds(0, SUB), :], tbuf.at[:, pl.ds(nr + SUB, SUB), :], 1, {"flow": f_prev})
    cor_dn = remote(corr_ref, corr_dn, 2, {"flow": f_next})
    cor_up = remote(corr_ref, corr_up, 3, {"flow": f_prev})
    for copy in (cor_dn, cor_up, row_dn, row_up):
        copy.start()

    layer = lax.broadcasted_iota(jnp.int32, (nl, nr), 0)
    column = lax.broadcasted_iota(jnp.int32, (nl, nr), 1)
    cats = [cat_ref[base + j] for j in range(nl)]
    catv = jnp.zeros((nl, nr), jnp.int32)
    for j in range(nl):
        catv = jnp.where(layer == j, cats[j], catv)
    corr = corr_ref[...]
    kind = catv * 4 + corr
    k_own = pick_pair(kind, PLANE_K)
    film = pick_pair(kind, FILM)
    level = jnp.where(catv == 0, LEVEL[0], jnp.where(catv == 1, LEVEL[1], LEVEL[2]))
    mass = 1.0 + film
    links = [link(scale, cats[j], cats[j + 1]) for j in range(nl - 1)]
    m = [mass[j : j + 1, :] for j in range(nl)]
    one, zero = jnp.ones((1, nr), jnp.float32), jnp.zeros((1, nr), jnp.float32)
    phi_ratio, psi_ratio = [None] * nl, [None] * nl
    up = m[nl - 2] + links[nl - 2]
    dn = m[1] + links[0]
    for j in range(nl - 2, 0, -1):
        inv = 1.0 / (up + links[j - 1])
        phi_ratio[j] = links[j - 1] * inv
        if j > 1:
            up = m[j - 1] + links[j - 1] * (up * inv)
        i = nl - 1 - j
        inv = 1.0 / (dn + links[i])
        psi_ratio[i] = links[i] * inv
        if i < nl - 2:
            dn = m[i + 1] + links[i] * (dn * inv)
    phi, psi = [one] + [None] * (nl - 2) + [zero], [zero] + [None] * (nl - 2) + [one]
    for j in range(1, nl - 1):
        phi[j] = phi[j - 1] * phi_ratio[j]
        i = nl - 1 - j
        psi[i] = psi[i + 1] * psi_ratio[i]
    gamma = links[0] * psi[1]
    g_a, g_b = m[0], m[nl - 1]
    for j in range(1, nl - 1):
        g_a = g_a + phi[j] * m[j]
        g_b = g_b + psi[j] * m[j]
    for j in range(nl):
        cbuf[j : j + 1, :] = phi[j]
        cbuf[nl + j : nl + j + 1, :] = psi[j]
    cbuf[5 * nl : 6 * nl, :] = film * level
    cbuf[6 * nl : 6 * nl + 1, :] = g_a
    cbuf[6 * nl + 1 : 6 * nl + 2, :] = g_b
    cbuf[6 * nl + 2 : 6 * nl + 3, :] = gamma
    cbuf[6 * nl + 3 : 6 * nl + 4, :] = 1.0 / gamma
    cbuf[6 * nl + 4 : LANES, :] = jnp.zeros((LANES - 6 * nl - 4, nr), jnp.float32)

    load.wait()
    slot = lax.broadcasted_iota(jnp.int32, (SUB, LANES), 1)

    @pl.loop(0, tiles)
    def _(rt):
        acc = jnp.zeros((SUB, LANES), jnp.float32)
        r = pl.multiple_of(rt * SUB, SUB)
        r1 = pl.multiple_of(r + SUB, SUB)
        for j in range(nl):
            acc = jnp.where(slot == j, lane(tbuf[j, pl.ds(r1, SUB), 0:LANES], 0, LANES), acc)
            acc = jnp.where(
                slot == nl + j,
                lane(tbuf[j, pl.ds(r1, SUB), nc - LANES : nc], LANES - 1, LANES),
                acc,
            )
        e_own[pl.ds(r, SUB), :] = acc

    edge_r = remote(e_own, e_left, 4, {"width": w_next})
    edge_l = remote(e_own, e_right, 5, {"width": w_prev})
    edge_r.start()
    edge_l.start()

    cor_dn.wait_recv()
    cor_up.wait_recv()
    k_dn = pick_pair(catv * 4 + corr_dn[...], PLANE_K)
    k_up = pick_pair(catv * 4 + corr_up[...], PLANE_K)
    last = column == nr - 1
    first = column == 0
    k_after = jnp.where(last, pltpu.roll(k_up, nr - 1, 1), pltpu.roll(k_own, nr - 1, 1))
    k_before = jnp.where(first, pltpu.roll(k_dn, 1, 1), pltpu.roll(k_own, 1, 1))
    c_up = INPLANE * face(k_own, k_after)
    c_dn = INPLANE * face(k_own, k_before)
    c_up = jnp.where(jnp.logical_and(last, fi == nf - 1), 0.0, c_up)
    c_dn = jnp.where(jnp.logical_and(first, fi == 0), 0.0, c_dn)
    cbuf[2 * nl : 3 * nl, :] = c_up
    cbuf[3 * nl : 4 * nl, :] = c_dn
    cbuf[4 * nl : 5 * nl, :] = INPLANE * k_own
    ct[...] = jnp.transpose(cbuf[...])

    def to_stack(src, dst, send, recv, dev):
        return pltpu.make_async_remote_copy(
            src_ref=src,
            dst_ref=dst.at[me],
            send_sem=send.at[dev],
            recv_sem=recv.at[me],
            device_id={"stack": dev},
            device_id_type=MESH,
        )

    @pl.loop(0, ns)
    def _(i):
        dev = lax.rem(me + half + i, ns)
        rows = ct.at[pl.ds(pl.multiple_of(dev * SUB, SUB), SUB), :]

        @pl.when(dev != me)
        def _():
            to_stack(rows, ct_rx, ct_send, ct_recv, dev).start()

        @pl.when(dev == me)
        def _():
            ct_rx[me] = rows[...]

    row_dn.wait_recv()
    row_up.wait_recv()
    edge_r.wait_recv()
    edge_l.wait_recv()

    wide = lax.broadcasted_iota(jnp.int32, (SUB, nc), 1)
    at_first, at_last = wide == 0, wide == nc - 1
    height = lax.broadcasted_iota(jnp.int32, (SUB, nc), 0)
    bottom, top = height == 0, height == SUB - 1

    @pl.loop(0, ns)
    def _(i):
        rt = lax.rem(me + half + i, ns)
        r = pl.multiple_of(rt * SUB, SUB)
        r1, r2 = pl.multiple_of(r + SUB, SUB), pl.multiple_of(r + 2 * SUB, SUB)
        co = ct[pl.ds(r, SUB), :]
        own = e_own[pl.ds(r, SUB), :]
        left = jnp.where(wi > 0, e_left[pl.ds(r, SUB), :], pltpu.roll(own, nl, 1))
        right = jnp.where(wi < nw - 1, e_right[pl.ds(r, SUB), :], pltpu.roll(own, LANES - nl, 1))
        rhs = []
        for j in range(nl):
            t = tbuf[j, pl.ds(r1, SUB), :]
            t_after = jnp.where(bottom, tbuf[j, pl.ds(r2, SUB), :], t)
            t_after = pltpu.roll(t_after, SUB - 1, 0)
            t_before = jnp.where(top, tbuf[j, pl.ds(r, SUB), :], t)
            t_before = pltpu.roll(t_before, 1, 0)
            t_right = jnp.where(at_last, lane(right, j, nc), pltpu.roll(t, nc - 1, 1))
            t_left = jnp.where(at_first, lane(left, nl + j, nc), pltpu.roll(t, 1, 1))
            value = t + lane(co, 2 * nl + j, nc) * (t_after - t)
            value = value + lane(co, 3 * nl + j, nc) * (t_before - t)
            value = value + lane(co, 4 * nl + j, nc) * ((t_right - t) + (t_left - t))
            rhs.append(value + lane(co, 5 * nl + j, nc))
        inv = lane(co, 6 * nl + 3, nc)
        fs = [lane(co, j, nc) for j in range(nl)]
        qs = [lane(co, nl + j, nc) for j in range(nl)]
        run = jnp.zeros((SUB, nc), jnp.float32)
        pre = [run]
        for j in range(1, nl - 1):
            run = run + qs[j] * rhs[j]
            pre.append(run)
        ld_b = run + rhs[nl - 1]
        out_ref[nl - 1, pl.ds(r, SUB), :] = jnp.zeros((SUB, nc), jnp.float32)
        run = jnp.zeros((SUB, nc), jnp.float32)
        for j in range(nl - 2, 0, -1):
            out_ref[j, pl.ds(r, SUB), :] = (fs[j] * pre[j] + qs[j] * run) * inv
            run = run + fs[j] * rhs[j]
        out_ref[0, pl.ds(r, SUB), :] = jnp.zeros((SUB, nc), jnp.float32)
        ld_a = run + rhs[0]

        @pl.when(rt != me)
        def _():
            ld_tx[rt, 0] = ld_a
            ld_tx[rt, 1] = ld_b
            to_stack(ld_tx.at[rt], ld_rx, ld_send, ld_recv, rt).start()

        @pl.when(rt == me)
        def _():
            ld_rx[me, 0] = ld_a
            ld_rx[me, 1] = ld_b

    def wait_from(dst, send, recv, dev):
        pltpu.make_async_remote_copy(
            src_ref=dst.at[dev],
            dst_ref=dst.at[dev],
            send_sem=send.at[dev],
            recv_sem=recv.at[dev],
            device_id={"stack": dev},
            device_id_type=MESH,
        ).wait_recv()

    @pl.loop(1, ns)
    def _(i):
        wait_from(ct_rx, ct_send, ct_recv, lax.rem(me + i, ns))

    ends = [(cat_ref[nl * d + nl - 1], cat_ref[nl * d + nl]) for d in range(ns - 1)]
    s = None
    for d in range(ns):
        co = ct_rx[d]
        g_lo, g_hi, gam = (lane(co, 6 * nl + q, LANES) for q in range(3))
        s = g_lo if d == 0 else g_lo + hold * s
        inv = 1.0 / (s + gam)
        piv[2 * d, 0] = inv
        hold = gam * inv
        piv[2 * d, 1] = hold
        s = g_hi + hold * s
        if d < ns - 1:
            outer = link(scale, *ends[d])
            inv = 1.0 / (s + outer)
            hold = outer * inv
        else:
            inv = 1.0 / s
            hold = jnp.zeros_like(inv)
        piv[2 * d + 1, 0] = inv
        piv[2 * d + 1, 1] = hold

    @pl.loop(1, ns)
    def _(i):
        wait_from(ld_rx, ld_send, ld_recv, lax.rem(me + i, ns))

    def spread(n, q):
        tile = piv[n, q]
        return jnp.concatenate([tile] * (nc // LANES), axis=1)

    flow = []
    for n in range(2 * ns):
        now = ld_rx[n // 2, n % 2]
        if n > 0:
            now = now + spread(n - 1, 1) * flow[n - 1]
        flow.append(now)
    x = None
    for n in range(2 * ns - 1, -1, -1):
        x = flow[n] * spread(n, 0) + (0.0 if x is None else spread(n, 1) * x)
        sol_tx[n // 2, n % 2] = x

    @pl.loop(0, ns)
    def _(i):
        dev = lax.rem(me + half + i, ns)

        @pl.when(dev != me)
        def _():
            to_stack(sol_tx.at[dev], sol_rx, sol_send, sol_recv, dev).start()

        @pl.when(dev == me)
        def _():
            sol_rx[me] = sol_tx[me]

    @pl.loop(0, ns)
    def _(i):
        rt = lax.rem(me + i, ns)

        @pl.when(rt != me)
        def _():
            wait_from(sol_rx, sol_send, sol_recv, rt)

        r = pl.multiple_of(rt * SUB, SUB)
        co = ct[pl.ds(r, SUB), :]
        lo, hi = sol_rx[rt, 0], sol_rx[rt, 1]
        for j in range(nl):
            old = out_ref[j, pl.ds(r, SUB), :]
            out_ref[j, pl.ds(r, SUB), :] = old + (lane(co, j, nc) * lo + lane(co, nl + j, nc) * hi)

    for copy in (row_dn, row_up, cor_dn, cor_up, edge_r, edge_l):
        copy.wait_send()

    @pl.loop(1, ns)
    def _(i):
        dev = lax.rem(me + i, ns)
        rows = ct.at[pl.ds(pl.multiple_of(dev * SUB, SUB), SUB), :]
        to_stack(rows, ct_rx, ct_send, ct_recv, dev).wait_send()
        to_stack(ld_tx.at[dev], ld_rx, ld_send, ld_recv, dev).wait_send()
        to_stack(sol_tx.at[dev], sol_rx, sol_send, sol_recv, dev).wait_send()


def per_device(initial_thermal_state, plate_fluid_category, corrugation_type_grid):
    nl, nr, nc = initial_thermal_state.shape
    ns, nf, nw = lax.axis_size("stack"), lax.axis_size("flow"), lax.axis_size("width")
    total = nl * ns
    scale = STACK_SCALE * float(total * total)
    dims = (ns, nf, nw, nl, nr, nc, scale)
    f32 = jnp.float32
    return pl.pallas_call(
        functools.partial(kernel, dims),
        out_shape=jax.ShapeDtypeStruct((nl, nr, nc), f32),
        in_specs=[
            pl.BlockSpec(memory_space=pltpu.SMEM),
            pl.BlockSpec(memory_space=pltpu.VMEM),
            pl.BlockSpec(memory_space=pl.ANY),
        ],
        out_specs=pl.BlockSpec(memory_space=pltpu.VMEM),
        scratch_shapes=[
            pltpu.VMEM((nl, nr + 2 * SUB, nc), f32),
            pltpu.VMEM((nr, LANES), f32),
            pltpu.VMEM((nr, LANES), f32),
            pltpu.VMEM((nr, LANES), f32),
            pltpu.VMEM((nl, nr), jnp.int32),
            pltpu.VMEM((nl, nr), jnp.int32),
            pltpu.VMEM((LANES, nr), f32),
            pltpu.VMEM((nr, LANES), f32),
            pltpu.VMEM((ns, SUB, LANES), f32),
            pltpu.VMEM((ns, 2, SUB, nc), f32),
            pltpu.VMEM((ns, 2, SUB, nc), f32),
            pltpu.VMEM((ns, 2, SUB, nc), f32),
            pltpu.VMEM((ns, 2, SUB, nc), f32),
            pltpu.VMEM((2 * ns, 2, SUB, LANES), f32),
            pltpu.SemaphoreType.DMA,
            pltpu.SemaphoreType.DMA((6,)),
            pltpu.SemaphoreType.DMA((6,)),
        ]
        + [pltpu.SemaphoreType.DMA((ns,))] * 6,
        compiler_params=pltpu.CompilerParams(collective_id=0, has_side_effects=True),
        name="stack_step",
    )(plate_fluid_category, corrugation_type_grid, initial_thermal_state)


def solution(mesh):
    placed = (P("stack", "flow", "width"), P(), P("stack", "flow"))
    return jax.shard_map(
        per_device,
        mesh=mesh,
        in_specs=placed,
        out_specs=P("stack", "flow", "width"),
        check_vma=False,
    )
```

```python
import functools

import jax
import jax.numpy as jnp
from jax import lax
from jax.experimental import pallas as pl
from jax.experimental.pallas import tpu as pltpu
from jax.sharding import PartitionSpec as P

STACK_K = (0.15, 0.25, 1.0)
PLANE_K = ((0.35, 0.5, 0.7, 0.9), (0.3, 0.45, 0.65, 0.85), (0.8, 0.9, 1.0, 0.95))
FILM = ((0.4, 0.8, 1.2, 1.6), (0.3, 0.6, 1.0, 1.4), (0.0, 0.0, 0.0, 0.0))
LEVEL = (1.5, -1.0, 0.0)
INPLANE = 0.24
STACK_SCALE = 0.2
MESH = pl.DeviceIdType.MESH
SUB = 8
LANES = 128
PACK = 4
VMEM_BYTES = 67043328


def face(a, b):
    return 2.0 * a * b / (a + b)


def pick_scalar(code, values):
    out = jnp.float32(values[-1])
    for i in range(len(values) - 2, -1, -1):
        out = jnp.where(code == i, jnp.float32(values[i]), out)
    return out


def pick_pair(index, table):
    flat = [v for row in table for v in row]
    out = jnp.full(index.shape, flat[-1], jnp.float32)
    for i in range(len(flat) - 2, -1, -1):
        if flat[i] != flat[-1]:
            out = jnp.where(index == i, jnp.float32(flat[i]), out)
    return out


def link(scale, first, second):
    rows = []
    for a in STACK_K:
        rows.append(pick_scalar(second, [scale * face(a, b) for b in STACK_K]))
    return jnp.where(first == 0, rows[0], jnp.where(first == 1, rows[1], rows[2]))


def lane(tile, q):
    return jnp.broadcast_to(tile[:, q : q + 1], (tile.shape[0], LANES))


def rows_of(tile):
    return pl.ds(pl.multiple_of(tile * SUB, SUB), SUB)


def kernel(
    dims,
    cat_ref,
    corr_ref,
    t_hbm,
    out_ref,
    tbuf,
    row_lo,
    row_hi,
    e_own,
    e_left,
    e_right,
    corr_dn,
    corr_up,
    comp_tx,
    comp_rx,
    cbuf,
    ct,
    ct_rx,
    bc,
    fold,
    pair_tx,
    pair_rx,
    inner,
    ld_tx,
    ld_rx,
    sol_tx,
    sol_rx,
    end_tx,
    ends_buf,
    piv,
    t_sem,
    near_send,
    near_recv,
    ct_send,
    ct_recv,
    pair_send,
    pair_recv,
    ld_send,
    ld_recv,
    sol_send,
    sol_recv,
    end_send,
    end_recv,
    ready,
):
    ns, nf, nw, nl, nr, nc, scale = dims
    nch, tiles, halves = ns // 2, nr // SUB, nc // LANES
    half = nch // 2
    me, fi, wi = lax.axis_index("stack"), lax.axis_index("flow"), lax.axis_index("width")
    chip, core = me // 2, lax.rem(me, 2)
    other = 1 - core
    partner = {"stack": 2 * chip + other}
    f_next, f_prev = {"flow": lax.rem(fi + 1, nf)}, {"flow": lax.rem(fi + nf - 1, nf)}
    w_next, w_prev = {"width": lax.rem(wi + 1, nw)}, {"width": lax.rem(wi + nw - 1, nw)}

    def at_chip(steps):
        return {"stack": lax.rem(me + 2 * (steps % nch), ns)}

    load = pltpu.make_async_copy(t_hbm, tbuf.at[:, pl.ds(SUB, nr), :], t_sem)
    load.start()

    barrier = pltpu.get_barrier_semaphore()
    near = (f_next, f_prev, w_next, w_prev, partner, at_chip(1), at_chip(-1))
    for dev in near:
        pl.semaphore_signal(barrier, inc=1, device_id=dev, device_id_type=MESH)

    def remote(src, dst, k, dev):
        return pltpu.make_async_remote_copy(
            src_ref=src,
            dst_ref=dst,
            send_sem=near_send.at[k],
            recv_sem=near_recv.at[k],
            device_id=dev,
            device_id_type=MESH,
        )

    layer = lax.broadcasted_iota(jnp.int32, (nl, nr), 0)
    column = lax.broadcasted_iota(jnp.int32, (nl, nr), 1)
    base = me * nl
    cats = [cat_ref[base + j] for j in range(nl)]
    catv = jnp.zeros((nl, nr), jnp.int32)
    for j in range(nl):
        catv = jnp.where(layer == j, cats[j], catv)
    kind = catv * 4 + corr_ref[...]
    k_own = pick_pair(kind, PLANE_K)
    film = pick_pair(kind, FILM)
    level = jnp.where(catv == 0, LEVEL[0], jnp.where(catv == 1, LEVEL[1], LEVEL[2]))
    mass = 1.0 + film
    links = [link(scale, cats[j], cats[j + 1]) for j in range(nl - 1)]
    m = [mass[j : j + 1, :] for j in range(nl)]
    one, zero = jnp.ones((1, nr), jnp.float32), jnp.zeros((1, nr), jnp.float32)
    phi_ratio, psi_ratio = [None] * nl, [None] * nl
    up = m[nl - 2] + links[nl - 2]
    dn = m[1] + links[0]
    for j in range(nl - 2, 0, -1):
        inv = 1.0 / (up + links[j - 1])
        phi_ratio[j] = links[j - 1] * inv
        if j > 1:
            up = m[j - 1] + links[j - 1] * (up * inv)
        i = nl - 1 - j
        inv = 1.0 / (dn + links[i])
        psi_ratio[i] = links[i] * inv
        if i < nl - 2:
            dn = m[i + 1] + links[i] * (dn * inv)
    phi, psi = [one] + [None] * (nl - 2) + [zero], [zero] + [None] * (nl - 2) + [one]
    for j in range(1, nl - 1):
        phi[j] = phi[j - 1] * phi_ratio[j]
        i = nl - 1 - j
        psi[i] = psi[i + 1] * psi_ratio[i]
    gamma = links[0] * psi[1]
    g_a, g_b = m[0], m[nl - 1]
    for j in range(1, nl - 1):
        g_a = g_a + phi[j] * m[j]
        g_b = g_b + psi[j] * m[j]
    comp_tx[0:1, :] = g_a
    comp_tx[1:2, :] = g_b
    comp_tx[2:3, :] = gamma
    comp_tx[3:SUB, :] = jnp.zeros((SUB - 3, nr), jnp.float32)

    pl.semaphore_wait(barrier, len(near))
    comp = remote(comp_tx, comp_rx, 6, partner)
    cor_dn = remote(corr_ref, corr_dn, 2, f_next)
    cor_up = remote(corr_ref, corr_up, 3, f_prev)
    row_dn = remote(t_hbm.at[:, pl.ds(nr - 1, 1), :], row_lo, 0, f_next)
    row_up = remote(t_hbm.at[:, pl.ds(0, 1), :], row_hi, 1, f_prev)
    for copy in (comp, cor_dn, cor_up, row_dn, row_up):
        copy.start()
    for steps in (1, -1):
        pl.semaphore_signal(ready.at[0], inc=1, device_id=at_chip(steps), device_id_type=MESH)

    load.wait()
    slot = lax.broadcasted_iota(jnp.int32, (SUB, LANES), 1)
    at_first, at_last = slot == 0, slot == LANES - 1
    height = lax.broadcasted_iota(jnp.int32, (SUB, LANES), 0)
    bottom, top = height == 0, height == SUB - 1
    span = LANES // PACK

    @pl.loop(0, tiles // PACK)
    def _(g):
        acc = [jnp.zeros((SUB, LANES), jnp.float32) for _ in range(2)]
        for side, (start, q) in enumerate(((0, 0), (nc - LANES, LANES - 1))):
            for s in range(PACK):
                r = rows_of(g * PACK + s + 1)
                for j in range(nl):
                    value = lane(tbuf[j, r, start : start + LANES], q)
                    acc[side] = jnp.where(slot == s * span + side * nl + j, value, acc[side])
        e_own[rows_of(g), :] = acc[0] + acc[1]

    edge_r = remote(e_own, e_left, 4, w_next)
    edge_l = remote(e_own, e_right, 5, w_prev)
    edge_r.start()
    edge_l.start()

    pl.semaphore_wait(ready.at[0], 2)
    if nch > 4:
        for steps in (2, -2):
            pl.semaphore_signal(ready.at[1], inc=1, device_id=at_chip(steps), device_id_type=MESH)

    def inplane(k_before, k_after):
        last, first = column == nr - 1, column == 0
        after = jnp.where(last, k_after, pltpu.roll(k_own, nr - 1, 1))
        before = jnp.where(first, k_before, pltpu.roll(k_own, 1, 1))
        c_up = INPLANE * face(k_own, after)
        c_dn = INPLANE * face(k_own, before)
        c_up = jnp.where(jnp.logical_and(last, fi == nf - 1), 0.0, c_up)
        c_dn = jnp.where(jnp.logical_and(first, fi == 0), 0.0, c_dn)
        c_lr = INPLANE * k_own
        cbuf[2 * nl : 3 * nl, :] = c_up
        cbuf[3 * nl : 4 * nl, :] = c_dn
        cbuf[4 * nl : 5 * nl, :] = 1.0 - ((c_up + c_dn) + 2.0 * c_lr)
        return c_lr

    for j in range(nl):
        cbuf[j : j + 1, :] = phi[j]
        cbuf[nl + j : nl + j + 1, :] = psi[j]
    cbuf[5 * nl : 6 * nl, :] = inplane(k_own, k_own)
    cbuf[6 * nl : 7 * nl, :] = film * level

    comp.wait_recv()
    theirs = [comp_rx[q : q + 1, :] for q in range(3)]
    low = [jnp.where(core == 0, a, b) for a, b in zip((g_a, g_b, gamma), theirs)]
    high = [jnp.where(core == 0, b, a) for a, b in zip((g_a, g_b, gamma), theirs)]
    mid = link(scale, cat_ref[2 * nl * chip + nl - 1], cat_ref[2 * nl * chip + nl])
    t_in = high[0] + high[2]
    t_inv = 1.0 / (t_in + mid)
    t_out = low[1] + mid * (t_in * t_inv)
    w_p = low[2] / (low[2] + t_out)
    w_q = w_p * (mid * t_inv)
    s_in = low[1] + low[2]
    s_inv = 1.0 / (s_in + mid)
    s_out = high[0] + mid * (s_in * s_inv)
    w_v = high[2] / (high[2] + s_out)
    w_u = w_v * (mid * s_inv)
    chip_gamma = low[2] * w_u
    chip_lo = low[0] + w_p * low[1] + w_q * high[0]
    chip_hi = high[1] + w_u * low[1] + w_v * high[0]
    extra = (
        1.0 / gamma,
        w_p,
        w_q,
        w_u,
        w_v,
        w_u / chip_gamma,
        w_q / chip_gamma,
        chip_lo,
        chip_hi,
        chip_gamma,
    )
    x0 = 7 * nl
    for q, value in enumerate(extra):
        cbuf[x0 + q : x0 + q + 1, :] = value
    cbuf[x0 + len(extra) : LANES, :] = jnp.zeros((LANES - x0 - len(extra), nr), jnp.float32)
    ct[...] = jnp.transpose(cbuf[...])

    for q in range(x0 + 7):

        @pl.loop(0, tiles, unroll=8 if tiles % 8 == 0 else 4)
        def _(rt):
            bc[q, rt] = lane(ct[rows_of(rt), :], q)

    cor_dn.wait_recv()
    cor_up.wait_recv()
    inplane(
        pltpu.roll(pick_pair(catv * 4 + corr_dn[...], PLANE_K), 1, 1),
        pltpu.roll(pick_pair(catv * 4 + corr_up[...], PLANE_K), nr - 1, 1),
    )
    edge_co = jnp.transpose(cbuf[...])
    for rt in (0, tiles - 1):
        for q in range(2 * nl, 5 * nl):
            bc[q, rt] = lane(edge_co[rt * SUB : rt * SUB + SUB, :], q)

    row_dn.wait_recv()
    row_up.wait_recv()
    for j in range(nl):
        tbuf[j, SUB - 1 : SUB, :] = row_lo[j]
        tbuf[j, nr + SUB : nr + SUB + 1, :] = row_hi[j]
    edge_r.wait_recv()
    edge_l.wait_recv()

    def block(rt):
        g, s = rt // PACK, lax.rem(rt, PACK)
        turn = lax.rem((PACK - s) * span, LANES)
        own = e_own[rows_of(g), :]
        left = jnp.where(wi > 0, e_left[rows_of(g), :], pltpu.roll(own, nl, 1))
        right = jnp.where(wi < nw - 1, e_right[rows_of(g), :], pltpu.roll(own, LANES - nl, 1))
        left, right = pltpu.roll(left, turn, 1), pltpu.roll(right, turn, 1)
        r0, r1, r2 = rows_of(rt), rows_of(rt + 1), rows_of(rt + 2)
        inv = bc[x0, rt]
        pre, run = [None] * halves, [None] * halves
        ld_a, ld_b = [None] * halves, [None] * halves
        for j in range(nl):
            ts = [tbuf[j, r1, h * LANES : (h + 1) * LANES] for h in range(halves)]
            fwd = [pltpu.roll(t, 1, 1) for t in ts]
            bwd = [pltpu.roll(t, LANES - 1, 1) for t in ts]
            from_l = [pltpu.roll(left, LANES - nl - j, 1)] + fwd[:-1]
            from_r = bwd[1:] + [pltpu.roll(right, LANES - 1 - j, 1)]
            f, p = bc[j, rt], bc[nl + j, rt]
            for h in range(halves):
                cols = slice(h * LANES, (h + 1) * LANES)
                t = ts[h]
                after = pltpu.roll(jnp.where(bottom, tbuf[j, r2, cols], t), SUB - 1, 0)
                before = pltpu.roll(jnp.where(top, tbuf[j, r0, cols], t), 1, 0)
                beside = jnp.where(at_first, from_l[h], fwd[h]) + jnp.where(at_last, from_r[h], bwd[h])
                rhs = bc[4 * nl + j, rt] * t + bc[6 * nl + j, rt]
                rhs = rhs + bc[2 * nl + j, rt] * after
                rhs = rhs + bc[3 * nl + j, rt] * before
                rhs = rhs + bc[5 * nl + j, rt] * beside
                if j == 0:
                    ld_a[h] = rhs
                elif j == nl - 1:
                    ld_b[h] = pre[h] + rhs
                else:
                    if j == 1:
                        value = jnp.zeros((SUB, LANES), jnp.float32)
                        pre[h], run[h] = p * rhs, f * rhs
                    else:
                        value = (f * pre[h] - p * run[h]) * inv
                        pre[h], run[h] = pre[h] + p * rhs, run[h] + f * rhs
                    out_ref[j, r0, cols] = value
        for h in range(halves):
            ld_a[h] = ld_a[h] + run[h]
            fold[rt, :, h * LANES : (h + 1) * LANES] = run[h] * inv
        return ld_a, ld_b

    def to_partner(src, dst, send, recv, k):
        return pltpu.make_async_remote_copy(
            src_ref=src.at[k],
            dst_ref=dst.at[k],
            send_sem=send.at[k],
            recv_sem=recv.at[k],
            device_id=partner,
            device_id_type=MESH,
        )

    def to_chip(src, dst, send, recv, k):
        return pltpu.make_async_remote_copy(
            src_ref=src,
            dst_ref=dst.at[chip],
            send_sem=send.at[k],
            recv_sem=recv.at[chip],
            device_id={"stack": 2 * k + core},
            device_id_type=MESH,
        )

    def from_chip(dst, send, recv, k):
        return pltpu.make_async_remote_copy(
            src_ref=dst.at[k],
            dst_ref=dst.at[k],
            send_sem=send.at[k],
            recv_sem=recv.at[k],
            device_id={"stack": 2 * k + core},
            device_id_type=MESH,
        )

    @pl.loop(0, nch)
    def _(i):
        k = lax.rem(chip + half + i, nch)
        ld_a, ld_b = block(2 * k + other)
        for h in range(halves):
            cols = slice(h * LANES, (h + 1) * LANES)
            pair_tx[k, 0, :, cols] = ld_a[h]
            pair_tx[k, 1, :, cols] = ld_b[h]
        to_partner(pair_tx, pair_rx, pair_send, pair_recv, k).start()

    if nch > 4:
        pl.semaphore_wait(ready.at[1], 2)

    @pl.loop(0, nch)
    def _(i):
        k = lax.rem(chip + half + i, nch)
        rows = ct.at[rows_of(2 * k + core), :]

        @pl.when(k != chip)
        def _():
            to_chip(rows, ct_rx, ct_send, ct_recv, k).start()

        @pl.when(k == chip)
        def _():
            ct_rx[k] = rows[...]

    @pl.loop(0, nch)
    def _(i):
        k = lax.rem(chip + half + i, nch)
        rt = 2 * k + core
        ld_a, ld_b = block(rt)
        to_partner(pair_tx, pair_rx, pair_send, pair_recv, k).wait_recv()
        p, q, u, v = (bc[x0 + 1 + n, rt] for n in range(4))
        for h in range(halves):
            cols = slice(h * LANES, (h + 1) * LANES)
            their_a, their_b = pair_rx[k, 0, :, cols], pair_rx[k, 1, :, cols]
            f_b = jnp.where(core == 0, ld_b[h], their_b)
            f_a = jnp.where(core == 0, their_a, ld_a[h])
            f_lo = jnp.where(core == 0, ld_a[h], their_a)
            f_hi = jnp.where(core == 0, their_b, ld_b[h])
            to_lo = p * f_b + q * f_a
            to_hi = u * f_b + v * f_a
            inner[k, 0, :, cols] = to_lo
            inner[k, 1, :, cols] = to_hi
            ld_tx[k, 0, :, cols] = f_lo + to_lo
            ld_tx[k, 1, :, cols] = f_hi + to_hi

        @pl.when(k != chip)
        def _():
            to_chip(ld_tx.at[k], ld_rx, ld_send, ld_recv, k).start()

        @pl.when(k == chip)
        def _():
            ld_rx[k] = ld_tx[k]

    @pl.loop(1, nch)
    def _(i):
        from_chip(ct_rx, ct_send, ct_recv, lax.rem(chip + i, nch)).wait_recv()

    s, hold = None, None
    for d in range(nch):
        g_lo, g_hi, gam = (lane(ct_rx[d], x0 + 7 + q) for q in range(3))
        s = g_lo if d == 0 else g_lo + hold * s
        inv = 1.0 / (s + gam)
        hold = gam * inv
        piv[2 * d, 0], piv[2 * d, 1] = inv, hold
        s = g_hi + hold * s
        if d < nch - 1:
            outer = link(scale, cat_ref[2 * nl * (d + 1) - 1], cat_ref[2 * nl * (d + 1)])
            inv = 1.0 / (s + outer)
            hold = outer * inv
        else:
            inv = 1.0 / s
            hold = jnp.zeros_like(inv)
        piv[2 * d + 1, 0], piv[2 * d + 1, 1] = inv, hold

    @pl.loop(1, nch)
    def _(i):
        from_chip(ld_rx, ld_send, ld_recv, lax.rem(chip + i, nch)).wait_recv()

    for h in range(halves):
        cols = slice(h * LANES, (h + 1) * LANES)
        flow = []
        for n in range(2 * nch):
            now = ld_rx[n // 2, n % 2, :, cols]
            if n > 0:
                now = now + piv[n - 1, 1] * flow[n - 1]
            flow.append(now)
        x = flow[-1] * piv[2 * nch - 1, 0]
        sol_tx[nch - 1, 1, :, cols] = x
        for n in range(2 * nch - 2, -1, -1):
            x = flow[n] * piv[n, 0] + piv[n, 1] * x
            sol_tx[n // 2, n % 2, :, cols] = x

    @pl.loop(0, nch)
    def _(i):
        k = lax.rem(chip + half + i, nch)

        @pl.when(k != chip)
        def _():
            to_chip(sol_tx.at[k], sol_rx, sol_send, sol_recv, k).start()

        @pl.when(k == chip)
        def _():
            sol_rx[k] = sol_tx[k]

    def finish(rt, lo, hi):
        r = rows_of(rt)
        for h in range(halves):
            cols = slice(h * LANES, (h + 1) * LANES)
            out_ref[0, r, cols] = lo[h]
            out_ref[nl - 1, r, cols] = hi[h]
            bent = hi[h] + fold[rt, :, cols]
            for j in range(1, nl - 1):
                ends = bc[j, rt] * lo[h] + bc[nl + j, rt] * bent
                out_ref[j, r, cols] = out_ref[j, r, cols] + ends

    @pl.loop(0, nch)
    def _(i):
        k = lax.rem(chip + i, nch)
        rt = 2 * k + core

        @pl.when(k != chip)
        def _():
            from_chip(sol_rx, sol_send, sol_recv, k).wait_recv()

        p, q, u, v, s_b, s_a = (bc[x0 + 1 + n, rt] for n in range(6))
        lo, hi = [None] * halves, [None] * halves
        for h in range(halves):
            cols = slice(h * LANES, (h + 1) * LANES)
            x_lo, x_hi = sol_rx[k, 0, :, cols], sol_rx[k, 1, :, cols]
            x_b = p * x_lo + u * x_hi + s_b * inner[k, 0, :, cols]
            x_a = q * x_lo + v * x_hi + s_a * inner[k, 1, :, cols]
            lo[h] = jnp.where(core == 0, x_lo, x_a)
            hi[h] = jnp.where(core == 0, x_b, x_hi)
            end_tx[k, 0, :, cols] = jnp.where(core == 0, x_a, x_lo)
            end_tx[k, 1, :, cols] = jnp.where(core == 0, x_hi, x_b)
        to_partner(end_tx, ends_buf, end_send, end_recv, k).start()
        finish(rt, lo, hi)

    @pl.loop(0, nch)
    def _(i):
        k = lax.rem(chip + i, nch)
        to_partner(end_tx, ends_buf, end_send, end_recv, k).wait_recv()
        lo = [ends_buf[k, 0, :, h * LANES : (h + 1) * LANES] for h in range(halves)]
        hi = [ends_buf[k, 1, :, h * LANES : (h + 1) * LANES] for h in range(halves)]
        finish(2 * k + other, lo, hi)

    for copy in (comp, row_dn, row_up, cor_dn, cor_up, edge_r, edge_l):
        copy.wait_send()

    @pl.loop(0, nch)
    def _(k):
        to_partner(pair_tx, pair_rx, pair_send, pair_recv, k).wait_send()
        to_partner(end_tx, ends_buf, end_send, end_recv, k).wait_send()

        @pl.when(k != chip)
        def _():
            to_chip(ct.at[rows_of(2 * k + core), :], ct_rx, ct_send, ct_recv, k).wait_send()
            to_chip(ld_tx.at[k], ld_rx, ld_send, ld_recv, k).wait_send()
            to_chip(sol_tx.at[k], sol_rx, sol_send, sol_recv, k).wait_send()


def copy_out(parts, x_ref, out_ref, sem):
    step = x_ref.shape[0] // parts
    copies = [
        pltpu.make_async_copy(
            x_ref.at[pl.ds(n * step, step)], out_ref.at[pl.ds(n * step, step)], sem.at[n]
        )
        for n in range(parts)
    ]
    for copy in copies:
        copy.start()
    for copy in copies:
        copy.wait()


def per_device(initial_thermal_state, plate_fluid_category, corrugation_type_grid):
    nl, nr, nc = initial_thermal_state.shape
    ns, nf, nw = lax.axis_size("stack"), lax.axis_size("flow"), lax.axis_size("width")
    nch, tiles = ns // 2, nr // SUB
    total = nl * ns
    scale = STACK_SCALE * float(total * total)
    dims = (ns, nf, nw, nl, nr, nc, scale)
    f32 = jnp.float32
    packed = (tiles // PACK * SUB, LANES)
    tile_pair = pltpu.VMEM((nch, 2, SUB, nc), f32)
    dma = pltpu.SemaphoreType.DMA
    result = pl.pallas_call(
        functools.partial(kernel, dims),
        out_shape=pltpu.VMEM((nl, nr, nc), f32),
        in_specs=[
            pl.BlockSpec(memory_space=pltpu.SMEM),
            pl.BlockSpec(memory_space=pltpu.VMEM),
            pl.BlockSpec(memory_space=pl.ANY),
        ],
        out_specs=pl.BlockSpec(memory_space=pltpu.VMEM),
        scratch_shapes=[
            pltpu.VMEM((nl, nr + 2 * SUB, nc), f32),
            pltpu.VMEM((nl, 1, nc), f32),
            pltpu.VMEM((nl, 1, nc), f32),
            pltpu.VMEM(packed, f32),
            pltpu.VMEM(packed, f32),
            pltpu.VMEM(packed, f32),
            pltpu.VMEM((nl, nr), jnp.int32),
            pltpu.VMEM((nl, nr), jnp.int32),
            pltpu.VMEM((SUB, nr), f32),
            pltpu.VMEM((SUB, nr), f32),
            pltpu.VMEM((LANES, nr), f32),
            pltpu.VMEM((nr, LANES), f32),
            pltpu.VMEM((nch, SUB, LANES), f32),
            pltpu.VMEM((7 * nl + 7, tiles, SUB, LANES), f32),
            pltpu.VMEM((tiles, SUB, nc), f32),
        ]
        + [tile_pair] * 9
        + [
            pltpu.VMEM((2 * nch, 2, SUB, LANES), f32),
            dma,
            dma((7,)),
            dma((7,)),
        ]
        + [dma((nch,))] * 10
        + [pltpu.SemaphoreType.REGULAR((2,))],
        compiler_params=pltpu.CompilerParams(
            collective_id=0,
            has_side_effects=True,
            vmem_limit_bytes=VMEM_BYTES - 4 * nl * nr * nc - (1 << 20),
        ),
        name="stack_step",
    )(plate_fluid_category, corrugation_type_grid, initial_thermal_state)
    parts = 4
    return pl.pallas_call(
        functools.partial(copy_out, parts),
        out_shape=jax.ShapeDtypeStruct((nl, nr, nc), f32),
        in_specs=[pl.BlockSpec(memory_space=pltpu.VMEM)],
        out_specs=pl.BlockSpec(memory_space=pl.ANY),
        scratch_shapes=[dma((parts,))],
        compiler_params=pltpu.CompilerParams(vmem_limit_bytes=1 << 20),
        name="copy_out",
    )(result)


def solution(mesh):
    placed = (P("stack", "flow", "width"), P(), P("stack", "flow"))
    return jax.shard_map(
        per_device,
        mesh=mesh,
        in_specs=placed,
        out_specs=P("stack", "flow", "width"),
        check_vma=False,
    )
```

```python
import functools

import jax
import jax.numpy as jnp
from jax import lax
from jax.experimental import pallas as pl
from jax.experimental.pallas import tpu as pltpu
from jax.sharding import PartitionSpec as P

STACK_K = (0.15, 0.25, 1.0)
PLANE_K = ((0.35, 0.5, 0.7, 0.9), (0.3, 0.45, 0.65, 0.85), (0.8, 0.9, 1.0, 0.95))
FILM = ((0.4, 0.8, 1.2, 1.6), (0.3, 0.6, 1.0, 1.4), (0.0, 0.0, 0.0, 0.0))
LEVEL = (1.5, -1.0, 0.0)
INPLANE = 0.24
STACK_SCALE = 0.2
MESH = pl.DeviceIdType.MESH
SUB = 8
LANES = 128
PACK = 4
VMEM_BYTES = 67043328
LOADS = 4


def face(a, b):
    return 2.0 * a * b / (a + b)


def pick_scalar(code, values):
    out = jnp.float32(values[-1])
    for i in range(len(values) - 2, -1, -1):
        out = jnp.where(code == i, jnp.float32(values[i]), out)
    return out


def pick_pair(index, table):
    flat = [v for row in table for v in row]
    out = jnp.full(index.shape, flat[-1], jnp.float32)
    for i in range(len(flat) - 2, -1, -1):
        if flat[i] != flat[-1]:
            out = jnp.where(index == i, jnp.float32(flat[i]), out)
    return out


def link(scale, first, second):
    rows = []
    for a in STACK_K:
        rows.append(pick_scalar(second, [scale * face(a, b) for b in STACK_K]))
    return jnp.where(first == 0, rows[0], jnp.where(first == 1, rows[1], rows[2]))


def lane(tile, q):
    return jnp.broadcast_to(tile[:, q : q + 1], (tile.shape[0], LANES))


def rows_of(tile):
    return pl.ds(pl.multiple_of(tile * SUB, SUB), SUB)


def kernel(
    dims,
    cat_ref,
    corr_ref,
    t_hbm,
    out_ref,
    tbuf,
    row_lo,
    row_hi,
    e_own,
    e_left,
    e_right,
    corr_dn,
    corr_up,
    comp_tx,
    comp_rx,
    cbuf,
    ct,
    ct_rx,
    bc,
    mc,
    fold,
    pair_tx,
    pair_rx,
    inner,
    ld_tx,
    ld_rx,
    sol_tx,
    sol_rx,
    end_tx,
    ends_buf,
    piv,
    t_sem,
    near_send,
    near_recv,
    ct_send,
    ct_recv,
    pair_send,
    pair_recv,
    ld_send,
    ld_recv,
    sol_send,
    sol_recv,
    end_send,
    end_recv,
    ready,
):
    ns, nf, nw, nl, nr, nc, scale = dims
    nch, tiles, halves = ns // 2, nr // SUB, nc // LANES
    half = nch // 2
    me, fi, wi = lax.axis_index("stack"), lax.axis_index("flow"), lax.axis_index("width")
    chip, core = me // 2, lax.rem(me, 2)
    other = 1 - core
    partner = {"stack": 2 * chip + other}
    f_next, f_prev = {"flow": lax.rem(fi + 1, nf)}, {"flow": lax.rem(fi + nf - 1, nf)}
    w_next, w_prev = {"width": lax.rem(wi + 1, nw)}, {"width": lax.rem(wi + nw - 1, nw)}

    def at_chip(steps):
        return {"stack": lax.rem(me + 2 * (steps % nch), ns)}

    part = nl // LOADS
    loads = [
        pltpu.make_async_copy(
            t_hbm.at[pl.ds(n * part, part)],
            tbuf.at[pl.ds(n * part, part), pl.ds(SUB, nr), :],
            t_sem.at[n],
        )
        for n in range(LOADS)
    ]
    for load in loads:
        load.start()

    barrier = pltpu.get_barrier_semaphore()
    near = (f_next, f_prev, w_next, w_prev, partner, at_chip(1), at_chip(-1))
    for dev in near:
        pl.semaphore_signal(barrier, inc=1, device_id=dev, device_id_type=MESH)

    def remote(src, dst, k, dev):
        return pltpu.make_async_remote_copy(
            src_ref=src,
            dst_ref=dst,
            send_sem=near_send.at[k],
            recv_sem=near_recv.at[k],
            device_id=dev,
            device_id_type=MESH,
        )

    layer = lax.broadcasted_iota(jnp.int32, (nl, nr), 0)
    column = lax.broadcasted_iota(jnp.int32, (nl, nr), 1)
    base = me * nl
    cats = [cat_ref[base + j] for j in range(nl)]
    catv = jnp.zeros((nl, nr), jnp.int32)
    for j in range(nl):
        catv = jnp.where(layer == j, cats[j], catv)
    kind = catv * 4 + corr_ref[...]
    k_own = pick_pair(kind, PLANE_K)
    film = pick_pair(kind, FILM)
    level = jnp.where(catv == 0, LEVEL[0], jnp.where(catv == 1, LEVEL[1], LEVEL[2]))
    mass = 1.0 + film
    links = [link(scale, cats[j], cats[j + 1]) for j in range(nl - 1)]
    m = [mass[j : j + 1, :] for j in range(nl)]
    one, zero = jnp.ones((1, nr), jnp.float32), jnp.zeros((1, nr), jnp.float32)
    phi_ratio, psi_ratio = [None] * nl, [None] * nl
    up = m[nl - 2] + links[nl - 2]
    dn = m[1] + links[0]
    for j in range(nl - 2, 0, -1):
        inv = 1.0 / (up + links[j - 1])
        phi_ratio[j] = links[j - 1] * inv
        if j > 1:
            up = m[j - 1] + links[j - 1] * (up * inv)
        i = nl - 1 - j
        inv = 1.0 / (dn + links[i])
        psi_ratio[i] = links[i] * inv
        if i < nl - 2:
            dn = m[i + 1] + links[i] * (dn * inv)
    phi, psi = [one] + [None] * (nl - 2) + [zero], [zero] + [None] * (nl - 2) + [one]
    for j in range(1, nl - 1):
        phi[j] = phi[j - 1] * phi_ratio[j]
        i = nl - 1 - j
        psi[i] = psi[i + 1] * psi_ratio[i]
    gamma = links[0] * psi[1]
    g_a, g_b = m[0], m[nl - 1]
    for j in range(1, nl - 1):
        g_a = g_a + phi[j] * m[j]
        g_b = g_b + psi[j] * m[j]
    comp_tx[0:1, :] = g_a
    comp_tx[1:2, :] = g_b
    comp_tx[2:3, :] = gamma
    comp_tx[3:SUB, :] = jnp.zeros((SUB - 3, nr), jnp.float32)

    pl.semaphore_wait(barrier, len(near))
    comp = remote(comp_tx, comp_rx, 6, partner)
    cor_dn = remote(corr_ref, corr_dn, 2, f_next)
    cor_up = remote(corr_ref, corr_up, 3, f_prev)
    row_dn = remote(t_hbm.at[:, pl.ds(nr - 1, 1), :], row_lo, 0, f_next)
    row_up = remote(t_hbm.at[:, pl.ds(0, 1), :], row_hi, 1, f_prev)
    for copy in (comp, cor_dn, cor_up, row_dn, row_up):
        copy.start()
    for steps in (1, -1):
        pl.semaphore_signal(ready.at[0], inc=1, device_id=at_chip(steps), device_id_type=MESH)

    for load in loads:
        load.wait()
    slot = lax.broadcasted_iota(jnp.int32, (SUB, LANES), 1)
    at_first, at_last = slot == 0, slot == LANES - 1
    height = lax.broadcasted_iota(jnp.int32, (SUB, LANES), 0)
    bottom, top = height == 0, height == SUB - 1
    span = LANES // PACK
    x0 = 5 * nl + 1

    @pl.loop(0, tiles // PACK)
    def _(g):
        acc = [jnp.zeros((SUB, LANES), jnp.float32) for _ in range(2)]
        for side, (start, q) in enumerate(((0, 0), (nc - LANES, LANES - 1))):
            for s in range(PACK):
                r = rows_of(g * PACK + s + 1)
                for j in range(nl):
                    to = s * span + side * nl + j
                    value = pltpu.roll(tbuf[j, r, start : start + LANES], (to - q) % LANES, 1)
                    acc[side] = jnp.where(slot == to, value, acc[side])
        e_own[rows_of(g), :] = acc[0] + acc[1]

    edge_r = remote(e_own, e_left, 4, w_next)
    edge_l = remote(e_own, e_right, 5, w_prev)
    edge_r.start()
    edge_l.start()

    last, first = column == nr - 1, column == 0
    k_next = pltpu.roll(k_own, nr - 1, 1)
    c_lr = INPLANE * k_own
    for j in range(nl):
        cbuf[j : j + 1, :] = phi[j]
        cbuf[nl + j : nl + j + 1, :] = psi[j]
    cbuf[2 * nl : 3 * nl, :] = INPLANE * face(k_own, k_next)
    cbuf[3 * nl : 4 * nl, :] = c_lr
    cbuf[4 * nl : 5 * nl, :] = film * level
    cbuf[5 * nl : 5 * nl + 1, :] = 1.0 / gamma
    cbuf[5 * nl + 1 : LANES, :] = jnp.zeros((LANES - 5 * nl - 1, nr), jnp.float32)
    ct[...] = jnp.transpose(cbuf[...])

    @pl.loop(0, tiles // PACK)
    def _(g):
        tile = [ct[rows_of(g * PACK + s), :] for s in range(PACK)]
        for q in range(5 * nl + 1):
            for s in range(PACK):
                bc[q, g * PACK + s] = lane(tile[s], q)
        for j in range(nl):
            for s in range(PACK):
                rt = g * PACK + s
                up = bc[2 * nl + j, rt]
                before = bc[2 * nl + j, jnp.maximum(rt - 1, 0)]
                dn = pltpu.roll(jnp.where(top, before, up), 1, 0)
                bc[x0 + j, rt] = dn
                bc[x0 + nl + j, rt] = 1.0 - ((up + dn) + 2.0 * bc[3 * nl + j, rt])

    comp.wait_recv()
    theirs = [comp_rx[q : q + 1, :] for q in range(3)]
    low = [jnp.where(core == 0, a, b) for a, b in zip((g_a, g_b, gamma), theirs)]
    high = [jnp.where(core == 0, b, a) for a, b in zip((g_a, g_b, gamma), theirs)]
    mid = link(scale, cat_ref[2 * nl * chip + nl - 1], cat_ref[2 * nl * chip + nl])
    t_in = high[0] + high[2]
    t_inv = 1.0 / (t_in + mid)
    t_out = low[1] + mid * (t_in * t_inv)
    w_p = low[2] / (low[2] + t_out)
    w_q = w_p * (mid * t_inv)
    s_in = low[1] + low[2]
    s_inv = 1.0 / (s_in + mid)
    s_out = high[0] + mid * (s_in * s_inv)
    w_v = high[2] / (high[2] + s_out)
    w_u = w_v * (mid * s_inv)
    chip_gamma = low[2] * w_u
    chip_lo = low[0] + w_p * low[1] + w_q * high[0]
    chip_hi = high[1] + w_u * low[1] + w_v * high[0]
    merge = (w_p, w_q, w_u, w_v, w_u / chip_gamma, w_q / chip_gamma)
    for q, value in enumerate(merge + (chip_lo, chip_hi, chip_gamma)):
        cbuf[q : q + 1, :] = value
    ct[...] = jnp.transpose(cbuf[...])
    for k in range(nch):
        tile = ct[rows_of(2 * k + core), :]
        for q in range(len(merge)):
            mc[q, k] = lane(tile, q)

    cor_dn.wait_recv()
    cor_up.wait_recv()
    k_dn = pick_pair(catv * 4 + corr_dn[...], PLANE_K)
    k_up = pick_pair(catv * 4 + corr_up[...], PLANE_K)
    c_dn = INPLANE * face(k_own, pltpu.roll(k_dn, 1, 1))
    c_up = INPLANE * face(k_own, pltpu.roll(k_up, nr - 1, 1))
    c_dn = jnp.where(fi == 0, 0.0, jnp.broadcast_to(c_dn[:, 0:1], (nl, LANES)))
    c_up = jnp.where(fi == nf - 1, 0.0, jnp.broadcast_to(c_up[:, nr - 1 : nr], (nl, LANES)))
    end = tiles - 1
    for j in range(nl):
        dn = jnp.where(bottom, c_dn[j : j + 1, :], bc[x0 + j, 0])
        bc[x0 + j, 0] = dn
        up = jnp.where(top, c_up[j : j + 1, :], bc[2 * nl + j, end])
        bc[2 * nl + j, end] = up
        bc[x0 + nl + j, 0] = 1.0 - ((bc[2 * nl + j, 0] + dn) + 2.0 * bc[3 * nl + j, 0])
        bc[x0 + nl + j, end] = 1.0 - ((up + bc[x0 + j, end]) + 2.0 * bc[3 * nl + j, end])

    pl.semaphore_wait(ready.at[0], 2)
    if nch > 4:
        for steps in (2, -2):
            pl.semaphore_signal(ready.at[1], inc=1, device_id=at_chip(steps), device_id_type=MESH)

    row_dn.wait_recv()
    row_up.wait_recv()
    for j in range(nl):
        tbuf[j, SUB - 1 : SUB, :] = row_lo[j]
        tbuf[j, nr + SUB : nr + SUB + 1, :] = row_hi[j]
    edge_r.wait_recv()
    edge_l.wait_recv()

    def block(rt):
        g, s = rt // PACK, lax.rem(rt, PACK)
        turn = lax.rem((PACK - s) * span, LANES)
        own = e_own[rows_of(g), :]
        left = jnp.where(wi > 0, e_left[rows_of(g), :], pltpu.roll(own, nl, 1))
        right = jnp.where(wi < nw - 1, e_right[rows_of(g), :], pltpu.roll(own, LANES - nl, 1))
        left, right = pltpu.roll(left, turn, 1), pltpu.roll(right, turn, 1)
        r0, r1, r2 = rows_of(rt), rows_of(rt + 1), rows_of(rt + 2)
        inv = bc[5 * nl, rt]
        pre, run = [None] * halves, [None] * halves
        ld_a, ld_b = [None] * halves, [None] * halves
        for j in range(nl):
            ts = [tbuf[j, r1, h * LANES : (h + 1) * LANES] for h in range(halves)]
            fwd = [pltpu.roll(t, 1, 1) for t in ts]
            bwd = [pltpu.roll(t, LANES - 1, 1) for t in ts]
            from_l = [pltpu.roll(left, LANES - nl - j, 1)] + fwd[:-1]
            from_r = bwd[1:] + [pltpu.roll(right, LANES - 1 - j, 1)]
            f, p = bc[j, rt], bc[nl + j, rt]
            for h in range(halves):
                cols = slice(h * LANES, (h + 1) * LANES)
                t = ts[h]
                after = pltpu.roll(jnp.where(bottom, tbuf[j, r2, cols], t), SUB - 1, 0)
                before = pltpu.roll(jnp.where(top, tbuf[j, r0, cols], t), 1, 0)
                beside = jnp.where(at_first, from_l[h], fwd[h]) + jnp.where(at_last, from_r[h], bwd[h])
                rhs = bc[x0 + nl + j, rt] * t + bc[4 * nl + j, rt]
                rhs = rhs + bc[2 * nl + j, rt] * after
                rhs = rhs + bc[x0 + j, rt] * before
                rhs = rhs + bc[3 * nl + j, rt] * beside
                if j == 0:
                    ld_a[h] = rhs
                elif j == nl - 1:
                    ld_b[h] = pre[h] + rhs
                else:
                    if j == 1:
                        value = jnp.zeros((SUB, LANES), jnp.float32)
                        pre[h], run[h] = p * rhs, f * rhs
                    else:
                        value = (f * pre[h] - p * run[h]) * inv
                        pre[h], run[h] = pre[h] + p * rhs, run[h] + f * rhs
                    out_ref[j, r0, cols] = value
        for h in range(halves):
            ld_a[h] = ld_a[h] + run[h]
            fold[rt, :, h * LANES : (h + 1) * LANES] = run[h] * inv
        return ld_a, ld_b

    def to_partner(src, dst, send, recv, k):
        return pltpu.make_async_remote_copy(
            src_ref=src.at[k],
            dst_ref=dst.at[k],
            send_sem=send,
            recv_sem=recv.at[k],
            device_id=partner,
            device_id_type=MESH,
        )

    def to_chip(src, dst, send, recv, k):
        return pltpu.make_async_remote_copy(
            src_ref=src,
            dst_ref=dst.at[chip],
            send_sem=send,
            recv_sem=recv,
            device_id={"stack": 2 * k + core},
            device_id_type=MESH,
        )

    def whole(ref, send, recv):
        return pltpu.make_async_remote_copy(
            src_ref=ref,
            dst_ref=ref,
            send_sem=send,
            recv_sem=recv,
            device_id=partner,
            device_id_type=MESH,
        )

    def inward(t):
        return [lax.rem(chip + nch - half + t, nch), lax.rem(chip + half - 1 - t, nch)]

    def outward(t):
        return [lax.rem(chip + t, nch), lax.rem(chip + nch - 1 - t, nch)]

    columns = [slice(h * LANES, (h + 1) * LANES) for h in range(halves)]

    @pl.loop(0, half)
    def _(t):
        ks = inward(t)
        found = [block(2 * k + other) for k in ks]
        for k, (ld_a, ld_b) in zip(ks, found):
            for h, cols in enumerate(columns):
                pair_tx[k, 0, :, cols] = ld_a[h]
                pair_tx[k, 1, :, cols] = ld_b[h]
            to_partner(pair_tx, pair_rx, pair_send, pair_recv, k).start()

    if nch > 4:
        pl.semaphore_wait(ready.at[1], 2)

    @pl.loop(1, nch)
    def _(i):
        k = lax.rem(chip + i, nch)
        to_chip(ct.at[rows_of(2 * k + core), :], ct_rx, ct_send, ct_recv, k).start()

    ct_rx[chip] = ct[rows_of(me), :]

    @pl.loop(0, half)
    def _(t):
        ks = inward(t)
        found = [block(2 * k + core) for k in ks]
        for k, (ld_a, ld_b) in zip(ks, found):
            to_partner(pair_tx, pair_rx, pair_send, pair_recv, k).wait_recv()
            p, q, u, v = (mc[n, k] for n in range(4))
            for h, cols in enumerate(columns):
                their_a, their_b = pair_rx[k, 0, :, cols], pair_rx[k, 1, :, cols]
                f_b = jnp.where(core == 0, ld_b[h], their_b)
                f_a = jnp.where(core == 0, their_a, ld_a[h])
                f_lo = jnp.where(core == 0, ld_a[h], their_a)
                f_hi = jnp.where(core == 0, their_b, ld_b[h])
                to_lo = p * f_b + q * f_a
                to_hi = u * f_b + v * f_a
                inner[k, 0, :, cols] = to_lo
                inner[k, 1, :, cols] = to_hi
                ld_tx[k, 0, :, cols] = f_lo + to_lo
                ld_tx[k, 1, :, cols] = f_hi + to_hi

            @pl.when(k != chip)
            def _():
                to_chip(ld_tx.at[k], ld_rx, ld_send, ld_recv, k).start()

    ld_rx[chip] = ld_tx[chip]

    others = pl.ds(0, nch - 1)
    whole(ct_rx.at[others], ct_send, ct_recv).wait_recv()
    s, hold = None, None
    for d in range(nch):
        g_lo, g_hi, gam = (lane(ct_rx[d], len(merge) + q) for q in range(3))
        s = g_lo if d == 0 else g_lo + hold * s
        inv = 1.0 / (s + gam)
        hold = gam * inv
        piv[2 * d, 0], piv[2 * d, 1] = inv, hold
        s = g_hi + hold * s
        if d < nch - 1:
            outer = link(scale, cat_ref[2 * nl * (d + 1) - 1], cat_ref[2 * nl * (d + 1)])
            inv = 1.0 / (s + outer)
            hold = outer * inv
        else:
            inv = 1.0 / s
            hold = jnp.zeros_like(inv)
        piv[2 * d + 1, 0], piv[2 * d + 1, 1] = inv, hold

    whole(ld_rx.at[others], ld_send, ld_recv).wait_recv()
    for cols in columns:
        flow = []
        for n in range(2 * nch):
            now = ld_rx[n // 2, n % 2, :, cols]
            if n > 0:
                now = now + piv[n - 1, 1] * flow[n - 1]
            flow.append(now)
        x = flow[-1] * piv[2 * nch - 1, 0]
        sol_tx[nch - 1, 1, :, cols] = x
        for n in range(2 * nch - 2, -1, -1):
            x = flow[n] * piv[n, 0] + piv[n, 1] * x
            sol_tx[n // 2, n % 2, :, cols] = x

    @pl.loop(0, nch - 1)
    def _(i):
        k = lax.rem(chip + half + i + (i >= half), nch)
        to_chip(sol_tx.at[k], sol_rx, sol_send, sol_recv.at[chip], k).start()

    sol_rx[chip] = sol_tx[chip]

    def finish(rt, lo, hi):
        r = rows_of(rt)
        for h, cols in enumerate(columns):
            out_ref[0, r, cols] = lo[h]
            out_ref[nl - 1, r, cols] = hi[h]
            bent = hi[h] + fold[rt, :, cols]
            for j in range(1, nl - 1):
                ends = bc[j, rt] * lo[h] + bc[nl + j, rt] * bent
                out_ref[j, r, cols] = out_ref[j, r, cols] + ends

    def finish_own(t):
        ks = outward(t)
        found = []
        for k in ks:

            @pl.when(k != chip)
            def _():
                to_chip(sol_tx.at[k], sol_rx, sol_send, sol_recv.at[k], k).wait_recv()

            p, q, u, v, s_b, s_a = (mc[n, k] for n in range(6))
            lo, hi = [None] * halves, [None] * halves
            for h, cols in enumerate(columns):
                x_lo, x_hi = sol_rx[k, 0, :, cols], sol_rx[k, 1, :, cols]
                x_b = p * x_lo + u * x_hi + s_b * inner[k, 0, :, cols]
                x_a = q * x_lo + v * x_hi + s_a * inner[k, 1, :, cols]
                lo[h] = jnp.where(core == 0, x_lo, x_a)
                hi[h] = jnp.where(core == 0, x_b, x_hi)
                end_tx[k, 0, :, cols] = jnp.where(core == 0, x_a, x_lo)
                end_tx[k, 1, :, cols] = jnp.where(core == 0, x_hi, x_b)
            to_partner(end_tx, ends_buf, end_send, end_recv, k).start()
            found.append((lo, hi))
        for k, (lo, hi) in zip(ks, found):
            finish(2 * k + core, lo, hi)

    def finish_theirs(t):
        ks = outward(t)
        for k in ks:
            to_partner(end_tx, ends_buf, end_send, end_recv, k).wait_recv()
        for k in ks:
            lo = [ends_buf[k, 0, :, cols] for cols in columns]
            hi = [ends_buf[k, 1, :, cols] for cols in columns]
            finish(2 * k + other, lo, hi)

    finish_own(0)

    @pl.loop(1, half)
    def _(t):
        finish_own(t)
        finish_theirs(t - 1)

    finish_theirs(half - 1)

    for copy in (comp, row_dn, row_up, cor_dn, cor_up, edge_r, edge_l):
        copy.wait_send()
    whole(pair_tx, pair_send, ct_recv).wait_send()
    whole(end_tx, end_send, ct_recv).wait_send()
    whole(ct_rx.at[others], ct_send, ct_recv).wait_send()
    whole(ld_tx.at[others], ld_send, ct_recv).wait_send()
    whole(sol_tx.at[others], sol_send, ct_recv).wait_send()


def copy_out(parts, x_ref, out_ref, sem):
    step = x_ref.shape[0] // parts
    copies = [
        pltpu.make_async_copy(
            x_ref.at[pl.ds(n * step, step)], out_ref.at[pl.ds(n * step, step)], sem.at[n]
        )
        for n in range(parts)
    ]
    for copy in copies:
        copy.start()
    for copy in copies:
        copy.wait()


def per_device(initial_thermal_state, plate_fluid_category, corrugation_type_grid):
    nl, nr, nc = initial_thermal_state.shape
    ns, nf, nw = lax.axis_size("stack"), lax.axis_size("flow"), lax.axis_size("width")
    nch, tiles = ns // 2, nr // SUB
    total = nl * ns
    scale = STACK_SCALE * float(total * total)
    dims = (ns, nf, nw, nl, nr, nc, scale)
    f32 = jnp.float32
    packed = (tiles // PACK * SUB, LANES)
    tile_pair = pltpu.VMEM((nch, 2, SUB, nc), f32)
    dma = pltpu.SemaphoreType.DMA
    result = pl.pallas_call(
        functools.partial(kernel, dims),
        out_shape=pltpu.VMEM((nl, nr, nc), f32),
        in_specs=[
            pl.BlockSpec(memory_space=pltpu.SMEM),
            pl.BlockSpec(memory_space=pltpu.VMEM),
            pl.BlockSpec(memory_space=pl.ANY),
        ],
        out_specs=pl.BlockSpec(memory_space=pltpu.VMEM),
        scratch_shapes=[
            pltpu.VMEM((nl, nr + 2 * SUB, nc), f32),
            pltpu.VMEM((nl, 1, nc), f32),
            pltpu.VMEM((nl, 1, nc), f32),
            pltpu.VMEM(packed, f32),
            pltpu.VMEM(packed, f32),
            pltpu.VMEM(packed, f32),
            pltpu.VMEM((nl, nr), jnp.int32),
            pltpu.VMEM((nl, nr), jnp.int32),
            pltpu.VMEM((SUB, nr), f32),
            pltpu.VMEM((SUB, nr), f32),
            pltpu.VMEM((LANES, nr), f32),
            pltpu.VMEM((nr, LANES), f32),
            pltpu.VMEM((nch, SUB, LANES), f32),
            pltpu.VMEM((7 * nl + 1, tiles, SUB, LANES), f32),
            pltpu.VMEM((6, nch, SUB, LANES), f32),
            pltpu.VMEM((tiles, SUB, nc), f32),
        ]
        + [tile_pair] * 9
        + [
            pltpu.VMEM((2 * nch, 2, SUB, LANES), f32),
            dma((LOADS,)),
            dma((7,)),
            dma((7,)),
            dma,
            dma,
            dma,
            dma((nch,)),
            dma,
            dma,
            dma,
            dma((nch,)),
            dma,
            dma((nch,)),
        ]
        + [pltpu.SemaphoreType.REGULAR((2,))],
        compiler_params=pltpu.CompilerParams(
            collective_id=0,
            has_side_effects=True,
            vmem_limit_bytes=VMEM_BYTES - 4 * nl * nr * nc - (1 << 20),
        ),
        name="stack_step",
    )(plate_fluid_category, corrugation_type_grid, initial_thermal_state)
    parts = 4
    return pl.pallas_call(
        functools.partial(copy_out, parts),
        out_shape=jax.ShapeDtypeStruct((nl, nr, nc), f32),
        in_specs=[pl.BlockSpec(memory_space=pltpu.VMEM)],
        out_specs=pl.BlockSpec(memory_space=pl.ANY),
        scratch_shapes=[dma((parts,))],
        compiler_params=pltpu.CompilerParams(vmem_limit_bytes=1 << 20),
        name="copy_out",
    )(result)


def solution(mesh):
    placed = (P("stack", "flow", "width"), P(), P("stack", "flow"))
    return jax.shard_map(
        per_device,
        mesh=mesh,
        in_specs=placed,
        out_specs=P("stack", "flow", "width"),
        check_vma=False,
    )
```

```python
import functools

import jax
import jax.numpy as jnp
from jax import lax
from jax.experimental import pallas as pl
from jax.experimental.pallas import tpu as pltpu
from jax.sharding import PartitionSpec as P

STACK_K = (0.15, 0.25, 1.0)
PLANE_K = ((0.35, 0.5, 0.7, 0.9), (0.3, 0.45, 0.65, 0.85), (0.8, 0.9, 1.0, 0.95))
FILM = ((0.4, 0.8, 1.2, 1.6), (0.3, 0.6, 1.0, 1.4), (0.0, 0.0, 0.0, 0.0))
LEVEL = (1.5, -1.0, 0.0)
INPLANE = 0.24
STACK_SCALE = 0.2
MESH = pl.DeviceIdType.MESH
SUB = 8
LANES = 128
PACK = 4
VMEM_BYTES = 67043328
LOADS = 4


def face(a, b):
    return 2.0 * a * b / (a + b)


def pick_scalar(code, values):
    out = jnp.float32(values[-1])
    for i in range(len(values) - 2, -1, -1):
        out = jnp.where(code == i, jnp.float32(values[i]), out)
    return out


def pick_pair(index, table):
    flat = [v for row in table for v in row]
    out = jnp.full(index.shape, flat[-1], jnp.float32)
    for i in range(len(flat) - 2, -1, -1):
        if flat[i] != flat[-1]:
            out = jnp.where(index == i, jnp.float32(flat[i]), out)
    return out


def link(scale, first, second):
    rows = []
    for a in STACK_K:
        rows.append(pick_scalar(second, [scale * face(a, b) for b in STACK_K]))
    return jnp.where(first == 0, rows[0], jnp.where(first == 1, rows[1], rows[2]))


def lane(tile, q):
    return jnp.broadcast_to(tile[:, q : q + 1], (tile.shape[0], LANES))


def rows_of(tile):
    return pl.ds(pl.multiple_of(tile * SUB, SUB), SUB)


def kernel(
    dims,
    cat_hbm,
    corr_hbm,
    t_hbm,
    out_ref,
    cat_ref,
    corr_ref,
    tbuf,
    row_lo,
    row_hi,
    e_own,
    e_left,
    e_right,
    corr_dn,
    corr_up,
    comp_tx,
    comp_rx,
    cbuf,
    ct,
    ct_rx,
    bc,
    mc,
    fold,
    pair_tx,
    pair_rx,
    inner,
    ld_tx,
    ld_rx,
    sol_tx,
    sol_rx,
    end_tx,
    ends_buf,
    piv,
    t_sem,
    near_send,
    near_recv,
    ct_send,
    ct_recv,
    pair_send,
    pair_recv,
    ld_send,
    ld_recv,
    sol_send,
    sol_recv,
    end_send,
    end_recv,
    ready,
):
    ns, nf, nw, nl, nr, nc, scale = dims
    nch, tiles, halves = ns // 2, nr // SUB, nc // LANES
    half = nch // 2
    me, fi, wi = lax.axis_index("stack"), lax.axis_index("flow"), lax.axis_index("width")
    chip, core = me // 2, lax.rem(me, 2)
    other = 1 - core
    partner = {"stack": 2 * chip + other}
    f_next, f_prev = {"flow": lax.rem(fi + 1, nf)}, {"flow": lax.rem(fi + nf - 1, nf)}
    w_next, w_prev = {"width": lax.rem(wi + 1, nw)}, {"width": lax.rem(wi + nw - 1, nw)}

    def at_chip(steps):
        return {"stack": lax.rem(me + 2 * (steps % nch), ns)}

    part = nl // LOADS
    loads = [
        pltpu.make_async_copy(
            t_hbm.at[pl.ds(n * part, part)],
            tbuf.at[pl.ds(n * part, part), pl.ds(SUB, nr), :],
            t_sem.at[n],
        )
        for n in range(LOADS)
    ]
    small = [
        pltpu.make_async_copy(cat_hbm, cat_ref, t_sem.at[LOADS]),
        pltpu.make_async_copy(corr_hbm, corr_ref, t_sem.at[LOADS + 1]),
    ]
    for load in small + loads:
        load.start()

    blank = jnp.zeros((SUB, nc), jnp.float32)
    for j in range(nl):
        tbuf[j, 0:SUB, :] = blank
        tbuf[j, nr + SUB : nr + 2 * SUB, :] = blank

    barrier = pltpu.get_barrier_semaphore()
    near = (f_next, f_prev, w_next, w_prev, partner, at_chip(1), at_chip(-1))
    for dev in near:
        pl.semaphore_signal(barrier, inc=1, device_id=dev, device_id_type=MESH)

    def remote(src, dst, k, dev):
        return pltpu.make_async_remote_copy(
            src_ref=src,
            dst_ref=dst,
            send_sem=near_send.at[k],
            recv_sem=near_recv.at[k],
            device_id=dev,
            device_id_type=MESH,
        )

    def to_chip(src, dst, send, recv, k):
        return pltpu.make_async_remote_copy(
            src_ref=src,
            dst_ref=dst.at[chip],
            send_sem=send,
            recv_sem=recv,
            device_id={"stack": 2 * k + core},
            device_id_type=MESH,
        )

    for copy in small:
        copy.wait()
    layer = lax.broadcasted_iota(jnp.int32, (nl, nr), 0)
    column = lax.broadcasted_iota(jnp.int32, (nl, nr), 1)
    base = me * nl
    cats = [cat_ref[base + j] for j in range(nl)]
    catv = jnp.zeros((nl, nr), jnp.int32)
    for j in range(nl):
        catv = jnp.where(layer == j, cats[j], catv)
    kind = catv * 4 + corr_ref[...]
    k_own = pick_pair(kind, PLANE_K)
    film = pick_pair(kind, FILM)
    level = jnp.where(catv == 0, LEVEL[0], jnp.where(catv == 1, LEVEL[1], LEVEL[2]))
    mass = 1.0 + film
    links = [link(scale, cats[j], cats[j + 1]) for j in range(nl - 1)]
    m = [mass[j : j + 1, :] for j in range(nl)]
    one, zero = jnp.ones((1, nr), jnp.float32), jnp.zeros((1, nr), jnp.float32)
    phi_ratio, psi_ratio = [None] * nl, [None] * nl
    up = m[nl - 2] + links[nl - 2]
    dn = m[1] + links[0]
    for j in range(nl - 2, 0, -1):
        inv = 1.0 / (up + links[j - 1])
        phi_ratio[j] = links[j - 1] * inv
        if j > 1:
            up = m[j - 1] + links[j - 1] * (up * inv)
        i = nl - 1 - j
        inv = 1.0 / (dn + links[i])
        psi_ratio[i] = links[i] * inv
        if i < nl - 2:
            dn = m[i + 1] + links[i] * (dn * inv)
    phi, psi = [one] + [None] * (nl - 2) + [zero], [zero] + [None] * (nl - 2) + [one]
    for j in range(1, nl - 1):
        phi[j] = phi[j - 1] * phi_ratio[j]
        i = nl - 1 - j
        psi[i] = psi[i + 1] * psi_ratio[i]
    gamma = links[0] * psi[1]
    g_a, g_b = m[0], m[nl - 1]
    for j in range(1, nl - 1):
        g_a = g_a + phi[j] * m[j]
        g_b = g_b + psi[j] * m[j]
    comp_tx[0:1, :] = g_a
    comp_tx[1:2, :] = g_b
    comp_tx[2:3, :] = gamma
    comp_tx[3:SUB, :] = jnp.zeros((SUB - 3, nr), jnp.float32)

    slot = lax.broadcasted_iota(jnp.int32, (SUB, LANES), 1)
    at_first, at_last = slot == 0, slot == LANES - 1
    height = lax.broadcasted_iota(jnp.int32, (SUB, LANES), 0)
    bottom, top = height == 0, height == SUB - 1
    span = LANES // PACK
    x0 = 5 * nl + 1
    u0 = 2 * nl + 1
    last, first = column == nr - 1, column == 0
    k_next = pltpu.roll(k_own, nr - 1, 1)
    c_lr = INPLANE * k_own
    for j in range(nl):
        cbuf[j : j + 1, :] = phi[j]
        cbuf[nl + j : nl + j + 1, :] = psi[j]
    cbuf[2 * nl + 1 : 3 * nl + 1, :] = INPLANE * face(k_own, k_next)
    cbuf[3 * nl + 1 : 4 * nl + 1, :] = c_lr
    cbuf[4 * nl + 1 : 5 * nl + 1, :] = film * level
    cbuf[2 * nl : 2 * nl + 1, :] = 1.0 / gamma
    cbuf[5 * nl + 1 : LANES, :] = jnp.zeros((LANES - 5 * nl - 1, nr), jnp.float32)
    ct[...] = jnp.transpose(cbuf[...])

    def spread(first_q, last_q):
        tile = [ct[rows_of(rt), :] for rt in range(tiles)]
        for q in range(first_q, last_q):
            for rt in range(tiles):
                bc[q, rt] = lane(tile[rt], q)

    spread(0, 2 * nl + 1)

    for load in loads:
        load.wait()

    @pl.loop(0, tiles // PACK)
    def _(g):
        acc = [jnp.zeros((SUB, LANES), jnp.float32) for _ in range(2)]
        for side, (start, q) in enumerate(((0, 0), (nc - LANES, LANES - 1))):
            for s in range(PACK):
                r = rows_of(g * PACK + s + 1)
                for j in range(nl):
                    to = s * span + side * nl + j
                    value = pltpu.roll(tbuf[j, r, start : start + LANES], (to - q) % LANES, 1)
                    acc[side] = jnp.where(slot == to, value, acc[side])
        e_own[rows_of(g), :] = acc[0] + acc[1]

    pl.semaphore_wait(barrier, len(near))
    comp = remote(comp_tx, comp_rx, 6, partner)
    cor_dn = remote(corr_ref, corr_dn, 2, f_next)
    cor_up = remote(corr_ref, corr_up, 3, f_prev)
    row_dn = remote(t_hbm.at[:, pl.ds(nr - 1, 1), :], row_lo, 0, f_next)
    row_up = remote(t_hbm.at[:, pl.ds(0, 1), :], row_hi, 1, f_prev)
    for copy in (comp, cor_dn, cor_up, row_dn, row_up):
        copy.start()
    for steps in (1, -1):
        pl.semaphore_signal(ready.at[0], inc=1, device_id=at_chip(steps), device_id_type=MESH)

    edge_r = remote(e_own, e_left, 4, w_next)
    edge_l = remote(e_own, e_right, 5, w_prev)
    edge_r.start()
    edge_l.start()

    tile = [ct[rows_of(rt), :] for rt in range(tiles)]
    for j in range(nl):
        ups = [lane(tile[rt], u0 + j) for rt in range(tiles)]
        sides = [lane(tile[rt], u0 + nl + j) for rt in range(tiles)]
        for rt in range(tiles):
            if rt == tiles - 1:
                ups[rt] = jnp.where(top, 0.0, ups[rt])
            dn = pltpu.roll(jnp.where(top, ups[rt - 1] if rt > 0 else 0.0, ups[rt]), 1, 0)
            bc[u0 + j, rt] = ups[rt]
            bc[u0 + nl + j, rt] = sides[rt]
            bc[x0 + j, rt] = dn
            bc[x0 + nl + j, rt] = 1.0 - ((ups[rt] + dn) + 2.0 * sides[rt])
    spread(u0 + 2 * nl, u0 + 3 * nl)

    pl.semaphore_wait(ready.at[0], 2)
    if nch > 4:
        for steps in (2, -2):
            pl.semaphore_signal(ready.at[1], inc=1, device_id=at_chip(steps), device_id_type=MESH)

    columns = [slice(h * LANES, (h + 1) * LANES) for h in range(halves)]

    def right_side(rt):
        r0, r1, r2 = rows_of(rt), rows_of(rt + 1), rows_of(rt + 2)
        for j in range(nl):
            ts = [tbuf[j, r1, cols] for cols in columns]
            fwd = [pltpu.roll(t, 1, 1) for t in ts]
            bwd = [pltpu.roll(t, LANES - 1, 1) for t in ts]
            from_l = [0.0] + fwd[:-1]
            from_r = bwd[1:] + [0.0]
            for h, cols in enumerate(columns):
                t = ts[h]
                after = pltpu.roll(jnp.where(bottom, tbuf[j, r2, cols], t), SUB - 1, 0)
                before = pltpu.roll(jnp.where(top, tbuf[j, r0, cols], t), 1, 0)
                beside = jnp.where(at_first, from_l[h], fwd[h]) + jnp.where(at_last, from_r[h], bwd[h])
                rhs = bc[x0 + nl + j, rt] * t + bc[u0 + 2 * nl + j, rt]
                rhs = rhs + bc[u0 + j, rt] * after
                rhs = rhs + bc[x0 + j, rt] * before
                out_ref[j, r0, cols] = rhs + bc[u0 + nl + j, rt] * beside

    comp.wait_recv()
    theirs = [comp_rx[q : q + 1, :] for q in range(3)]
    low = [jnp.where(core == 0, a, b) for a, b in zip((g_a, g_b, gamma), theirs)]
    high = [jnp.where(core == 0, b, a) for a, b in zip((g_a, g_b, gamma), theirs)]
    mid = link(scale, cat_ref[2 * nl * chip + nl - 1], cat_ref[2 * nl * chip + nl])
    t_in = high[0] + high[2]
    t_inv = 1.0 / (t_in + mid)
    t_out = low[1] + mid * (t_in * t_inv)
    w_p = low[2] / (low[2] + t_out)
    w_q = w_p * (mid * t_inv)
    s_in = low[1] + low[2]
    s_inv = 1.0 / (s_in + mid)
    s_out = high[0] + mid * (s_in * s_inv)
    w_v = high[2] / (high[2] + s_out)
    w_u = w_v * (mid * s_inv)
    chip_gamma = low[2] * w_u
    chip_lo = low[0] + w_p * low[1] + w_q * high[0]
    chip_hi = high[1] + w_u * low[1] + w_v * high[0]
    merge = (w_p, w_q, w_u, w_v, w_u / chip_gamma, w_q / chip_gamma)
    for q, value in enumerate(merge + (chip_lo, chip_hi, chip_gamma)):
        cbuf[q : q + 1, :] = value
    ct[...] = jnp.transpose(cbuf[...])
    for k in range(nch):
        tile = ct[rows_of(2 * k + core), :]
        for q in range(len(merge)):
            mc[q, k] = lane(tile, q)

    @pl.loop(0, tiles // 2)
    def _(i):
        right_side(2 * i)
        right_side(2 * i + 1)

    if nch > 4:
        pl.semaphore_wait(ready.at[1], 2)

    @pl.loop(1, nch)
    def _(i):
        k = lax.rem(chip + i, nch)
        to_chip(ct.at[rows_of(2 * k + core), :], ct_rx, ct_send, ct_recv, k).start()

    ct_rx[chip] = ct[rows_of(me), :]

    cor_dn.wait_recv()
    cor_up.wait_recv()
    k_dn = pick_pair(catv * 4 + corr_dn[...], PLANE_K)
    k_up = pick_pair(catv * 4 + corr_up[...], PLANE_K)
    c_dn = INPLANE * face(k_own, pltpu.roll(k_dn, 1, 1))
    c_up = INPLANE * face(k_own, pltpu.roll(k_up, nr - 1, 1))
    c_dn = jnp.where(fi == 0, 0.0, jnp.broadcast_to(c_dn[:, 0:1], (nl, LANES)))
    c_up = jnp.where(fi == nf - 1, 0.0, jnp.broadcast_to(c_up[:, nr - 1 : nr], (nl, LANES)))
    row_dn.wait_recv()
    row_up.wait_recv()
    for j in range(nl):
        for cols in columns:
            for r, here, co, row in ((0, bottom, c_dn, row_lo), (nr - SUB, top, c_up, row_hi)):
                step = row[j, :, cols] - tbuf[j, r + SUB : r + 2 * SUB, cols]
                step = jnp.where(here, co[j : j + 1, :] * step, 0.0)
                out_ref[j, r : r + SUB, cols] = out_ref[j, r : r + SUB, cols] + step
    edge_r.wait_recv()
    edge_l.wait_recv()

    def block(rt):
        g, s = rt // PACK, lax.rem(rt, PACK)
        turn = lax.rem((PACK - s) * span, LANES)
        own = e_own[rows_of(g), :]
        left = jnp.where(wi > 0, e_left[rows_of(g), :], pltpu.roll(own, nl, 1))
        right = jnp.where(wi < nw - 1, e_right[rows_of(g), :], pltpu.roll(own, LANES - nl, 1))
        left, right = pltpu.roll(left, turn, 1), pltpu.roll(right, turn, 1)
        r0 = rows_of(rt)
        inv = bc[2 * nl, rt]
        pre, run = [None] * halves, [None] * halves
        ld_a, ld_b = [None] * halves, [None] * halves
        for j in range(nl):
            f, p, c_lr = bc[j, rt], bc[nl + j, rt], bc[u0 + nl + j, rt]
            for h, cols in enumerate(columns):
                rhs = out_ref[j, r0, cols]
                if h == 0:
                    edge = pltpu.roll(left, LANES - nl - j, 1)
                    rhs = rhs + jnp.where(at_first, c_lr * edge, 0.0)
                if h == halves - 1:
                    edge = pltpu.roll(right, LANES - 1 - j, 1)
                    rhs = rhs + jnp.where(at_last, c_lr * edge, 0.0)
                if j == 0:
                    ld_a[h] = rhs
                elif j == nl - 1:
                    ld_b[h] = pre[h] + rhs
                else:
                    if j == 1:
                        value = jnp.zeros((SUB, LANES), jnp.float32)
                        pre[h], run[h] = p * rhs, f * rhs
                    else:
                        value = (f * pre[h] - p * run[h]) * inv
                        pre[h], run[h] = pre[h] + p * rhs, run[h] + f * rhs
                    out_ref[j, r0, cols] = value
        for h in range(halves):
            ld_a[h] = ld_a[h] + run[h]
            fold[rt, :, h * LANES : (h + 1) * LANES] = run[h] * inv
        return ld_a, ld_b

    def to_partner(src, dst, send, recv, k):
        return pltpu.make_async_remote_copy(
            src_ref=src.at[k],
            dst_ref=dst.at[k],
            send_sem=send,
            recv_sem=recv.at[k],
            device_id=partner,
            device_id_type=MESH,
        )

    def whole(ref, send, recv):
        return pltpu.make_async_remote_copy(
            src_ref=ref,
            dst_ref=ref,
            send_sem=send,
            recv_sem=recv,
            device_id=partner,
            device_id_type=MESH,
        )

    def inward(t):
        return [lax.rem(chip + nch - half + t, nch), lax.rem(chip + half - 1 - t, nch)]

    def outward(t):
        return [lax.rem(chip + t, nch), lax.rem(chip + nch - 1 - t, nch)]

    def for_partner(t):
        ks = inward(t)
        found = [block(2 * k + other) for k in ks]
        for k, (ld_a, ld_b) in zip(ks, found):
            for h, cols in enumerate(columns):
                pair_tx[k, 0, :, cols] = ld_a[h]
                pair_tx[k, 1, :, cols] = ld_b[h]
            to_partner(pair_tx, pair_rx, pair_send, pair_recv, k).start()

    def for_chip(t):
        ks = inward(t)
        found = [block(2 * k + core) for k in ks]
        for k, (ld_a, ld_b) in zip(ks, found):
            to_partner(pair_tx, pair_rx, pair_send, pair_recv, k).wait_recv()
            p, q, u, v = (mc[n, k] for n in range(4))
            for h, cols in enumerate(columns):
                their_a, their_b = pair_rx[k, 0, :, cols], pair_rx[k, 1, :, cols]
                f_b = jnp.where(core == 0, ld_b[h], their_b)
                f_a = jnp.where(core == 0, their_a, ld_a[h])
                f_lo = jnp.where(core == 0, ld_a[h], their_a)
                f_hi = jnp.where(core == 0, their_b, ld_b[h])
                to_lo = p * f_b + q * f_a
                to_hi = u * f_b + v * f_a
                inner[k, 0, :, cols] = to_lo
                inner[k, 1, :, cols] = to_hi
                ld_tx[k, 0, :, cols] = f_lo + to_lo
                ld_tx[k, 1, :, cols] = f_hi + to_hi

            @pl.when(k != chip)
            def _():
                to_chip(ld_tx.at[k], ld_rx, ld_send, ld_recv, k).start()

    for_partner(0)

    @pl.loop(1, half)
    def _(t):
        for_partner(t)
        for_chip(t - 1)

    for_chip(half - 1)
    ld_rx[chip] = ld_tx[chip]

    others = pl.ds(0, nch - 1)
    whole(ct_rx.at[others], ct_send, ct_recv).wait_recv()
    s, hold = None, None
    for d in range(nch):
        g_lo, g_hi, gam = (lane(ct_rx[d], len(merge) + q) for q in range(3))
        s = g_lo if d == 0 else g_lo + hold * s
        inv = 1.0 / (s + gam)
        hold = gam * inv
        piv[2 * d, 0], piv[2 * d, 1] = inv, hold
        s = g_hi + hold * s
        if d < nch - 1:
            outer = link(scale, cat_ref[2 * nl * (d + 1) - 1], cat_ref[2 * nl * (d + 1)])
            inv = 1.0 / (s + outer)
            hold = outer * inv
        else:
            inv = 1.0 / s
            hold = jnp.zeros_like(inv)
        piv[2 * d + 1, 0], piv[2 * d + 1, 1] = inv, hold

    whole(ld_rx.at[others], ld_send, ld_recv).wait_recv()
    for cols in columns:
        flow = []
        for n in range(2 * nch):
            now = ld_rx[n // 2, n % 2, :, cols]
            if n > 0:
                now = now + piv[n - 1, 1] * flow[n - 1]
            flow.append(now)
        x = flow[-1] * piv[2 * nch - 1, 0]
        sol_tx[nch - 1, 1, :, cols] = x
        for n in range(2 * nch - 2, -1, -1):
            x = flow[n] * piv[n, 0] + piv[n, 1] * x
            sol_tx[n // 2, n % 2, :, cols] = x

    @pl.loop(0, nch - 1)
    def _(i):
        steps = (half - (i + 1) // 2) * (1 - 2 * lax.rem(i, 2))
        k = lax.rem(chip + nch + steps, nch)
        to_chip(sol_tx.at[k], sol_rx, sol_send, sol_recv.at[chip], k).start()

    sol_rx[chip] = sol_tx[chip]

    def finish(rt, lo, hi):
        r = rows_of(rt)
        for h, cols in enumerate(columns):
            out_ref[0, r, cols] = lo[h]
            out_ref[nl - 1, r, cols] = hi[h]
            bent = hi[h] + fold[rt, :, cols]
            for j in range(1, nl - 1):
                ends = bc[j, rt] * lo[h] + bc[nl + j, rt] * bent
                out_ref[j, r, cols] = out_ref[j, r, cols] + ends

    def finish_own(t):
        ks = outward(t)
        found = []
        for k in ks:

            @pl.when(k != chip)
            def _():
                to_chip(sol_tx.at[k], sol_rx, sol_send, sol_recv.at[k], k).wait_recv()

            p, q, u, v, s_b, s_a = (mc[n, k] for n in range(6))
            lo, hi = [None] * halves, [None] * halves
            for h, cols in enumerate(columns):
                x_lo, x_hi = sol_rx[k, 0, :, cols], sol_rx[k, 1, :, cols]
                x_b = p * x_lo + u * x_hi + s_b * inner[k, 0, :, cols]
                x_a = q * x_lo + v * x_hi + s_a * inner[k, 1, :, cols]
                lo[h] = jnp.where(core == 0, x_lo, x_a)
                hi[h] = jnp.where(core == 0, x_b, x_hi)
                end_tx[k, 0, :, cols] = jnp.where(core == 0, x_a, x_lo)
                end_tx[k, 1, :, cols] = jnp.where(core == 0, x_hi, x_b)
            to_partner(end_tx, ends_buf, end_send, end_recv, k).start()
            found.append((lo, hi))
        for k, (lo, hi) in zip(ks, found):
            finish(2 * k + core, lo, hi)

    def finish_theirs(t):
        ks = outward(t)
        for k in ks:
            to_partner(end_tx, ends_buf, end_send, end_recv, k).wait_recv()
        for k in ks:
            lo = [ends_buf[k, 0, :, cols] for cols in columns]
            hi = [ends_buf[k, 1, :, cols] for cols in columns]
            finish(2 * k + other, lo, hi)

    finish_own(0)

    @pl.loop(1, half)
    def _(t):
        finish_own(t)
        finish_theirs(t - 1)

    finish_theirs(half - 1)

    for copy in (comp, row_dn, row_up, cor_dn, cor_up, edge_r, edge_l):
        copy.wait_send()
    whole(pair_tx, pair_send, ct_recv).wait_send()
    whole(end_tx, end_send, ct_recv).wait_send()
    whole(ct_rx.at[others], ct_send, ct_recv).wait_send()
    whole(ld_tx.at[others], ld_send, ct_recv).wait_send()
    whole(sol_tx.at[others], sol_send, ct_recv).wait_send()


def copy_out(parts, x_ref, out_ref, sem):
    step = x_ref.shape[0] // parts
    copies = [
        pltpu.make_async_copy(
            x_ref.at[pl.ds(n * step, step)], out_ref.at[pl.ds(n * step, step)], sem.at[n]
        )
        for n in range(parts)
    ]
    for copy in copies:
        copy.start()
    for copy in copies:
        copy.wait()


def per_device(initial_thermal_state, plate_fluid_category, corrugation_type_grid):
    nl, nr, nc = initial_thermal_state.shape
    ns, nf, nw = lax.axis_size("stack"), lax.axis_size("flow"), lax.axis_size("width")
    nch, tiles = ns // 2, nr // SUB
    total = nl * ns
    scale = STACK_SCALE * float(total * total)
    dims = (ns, nf, nw, nl, nr, nc, scale)
    f32 = jnp.float32
    packed = (tiles // PACK * SUB, LANES)
    tile_pair = pltpu.VMEM((nch, 2, SUB, nc), f32)
    dma = pltpu.SemaphoreType.DMA
    result = pl.pallas_call(
        functools.partial(kernel, dims),
        out_shape=pltpu.VMEM((nl, nr, nc), f32),
        in_specs=[
            pl.BlockSpec(memory_space=pl.ANY),
            pl.BlockSpec(memory_space=pl.ANY),
            pl.BlockSpec(memory_space=pl.ANY),
        ],
        out_specs=pl.BlockSpec(memory_space=pltpu.VMEM),
        scratch_shapes=[
            pltpu.SMEM((total,), jnp.int32),
            pltpu.VMEM((nl, nr), jnp.int32),
            pltpu.VMEM((nl, nr + 2 * SUB, nc), f32),
            pltpu.VMEM((nl, 1, nc), f32),
            pltpu.VMEM((nl, 1, nc), f32),
            pltpu.VMEM(packed, f32),
            pltpu.VMEM(packed, f32),
            pltpu.VMEM(packed, f32),
            pltpu.VMEM((nl, nr), jnp.int32),
            pltpu.VMEM((nl, nr), jnp.int32),
            pltpu.VMEM((SUB, nr), f32),
            pltpu.VMEM((SUB, nr), f32),
            pltpu.VMEM((LANES, nr), f32),
            pltpu.VMEM((nr, LANES), f32),
            pltpu.VMEM((nch, SUB, LANES), f32),
            pltpu.VMEM((7 * nl + 1, tiles, SUB, LANES), f32),
            pltpu.VMEM((6, nch, SUB, LANES), f32),
            pltpu.VMEM((tiles, SUB, nc), f32),
        ]
        + [tile_pair] * 9
        + [
            pltpu.VMEM((2 * nch, 2, SUB, LANES), f32),
            dma((LOADS + 2,)),
            dma((7,)),
            dma((7,)),
            dma,
            dma,
            dma,
            dma((nch,)),
            dma,
            dma,
            dma,
            dma((nch,)),
            dma,
            dma((nch,)),
        ]
        + [pltpu.SemaphoreType.REGULAR((2,))],
        compiler_params=pltpu.CompilerParams(
            collective_id=0,
            has_side_effects=True,
            vmem_limit_bytes=VMEM_BYTES - 4 * nl * nr * nc - (1 << 20),
        ),
        name="stack_step",
    )(plate_fluid_category, corrugation_type_grid, initial_thermal_state)
    parts = 4
    return pl.pallas_call(
        functools.partial(copy_out, parts),
        out_shape=jax.ShapeDtypeStruct((nl, nr, nc), f32),
        in_specs=[pl.BlockSpec(memory_space=pltpu.VMEM)],
        out_specs=pl.BlockSpec(memory_space=pl.ANY),
        scratch_shapes=[dma((parts,))],
        compiler_params=pltpu.CompilerParams(vmem_limit_bytes=1 << 20),
        name="copy_out",
    )(result)


def solution(mesh):
    placed = (P("stack", "flow", "width"), P(), P("stack", "flow"))
    return jax.shard_map(
        per_device,
        mesh=mesh,
        in_specs=placed,
        out_specs=P("stack", "flow", "width"),
        check_vma=False,
    )
```

```python
import functools

import jax
import jax.numpy as jnp
from jax import lax
from jax.experimental import pallas as pl
from jax.experimental.pallas import tpu as pltpu
from jax.sharding import PartitionSpec as P

STACK_K = (0.15, 0.25, 1.0)
PLANE_K = ((0.35, 0.5, 0.7, 0.9), (0.3, 0.45, 0.65, 0.85), (0.8, 0.9, 1.0, 0.95))
FILM = ((0.4, 0.8, 1.2, 1.6), (0.3, 0.6, 1.0, 1.4), (0.0, 0.0, 0.0, 0.0))
LEVEL = (1.5, -1.0, 0.0)
INPLANE = 0.24
STACK_SCALE = 0.2
MESH = pl.DeviceIdType.MESH
SUB = 8
LANES = 128
PACK = 4
VMEM_BYTES = 67043328
LOADS = 4


def face(a, b):
    return 2.0 * a * b / (a + b)


def pick_scalar(code, values):
    out = jnp.float32(values[-1])
    for i in range(len(values) - 2, -1, -1):
        out = jnp.where(code == i, jnp.float32(values[i]), out)
    return out


def pick_pair(index, table):
    flat = [v for row in table for v in row]
    out = jnp.full(index.shape, flat[-1], jnp.float32)
    for i in range(len(flat) - 2, -1, -1):
        if flat[i] != flat[-1]:
            out = jnp.where(index == i, jnp.float32(flat[i]), out)
    return out


def link(scale, first, second):
    rows = []
    for a in STACK_K:
        rows.append(pick_scalar(second, [scale * face(a, b) for b in STACK_K]))
    return jnp.where(first == 0, rows[0], jnp.where(first == 1, rows[1], rows[2]))


def lane(tile, q):
    return jnp.broadcast_to(tile[:, q : q + 1], (tile.shape[0], LANES))


def rows_of(tile):
    return pl.ds(pl.multiple_of(tile * SUB, SUB), SUB)


def kernel(
    dims,
    cat_hbm,
    corr_hbm,
    t_hbm,
    out_ref,
    cat_ref,
    corr_ref,
    tbuf,
    row_lo,
    row_hi,
    e_own,
    e_left,
    e_right,
    corr_dn,
    corr_up,
    comp_tx,
    comp_rx,
    cbuf,
    ct,
    ct_rx,
    bc,
    mc,
    fold,
    pair_tx,
    pair_rx,
    inner,
    ld_tx,
    ld_rx,
    sol_tx,
    sol_rx,
    end_tx,
    ends_buf,
    piv,
    t_sem,
    near_send,
    near_recv,
    ct_send,
    ct_recv,
    pair_send,
    pair_recv,
    ld_send,
    ld_recv,
    sol_send,
    sol_recv,
    end_send,
    end_recv,
    ready,
):
    ns, nf, nw, nl, nr, nc, scale = dims
    nch, tiles, halves = ns // 2, nr // SUB, nc // LANES
    half = nch // 2
    me, fi, wi = lax.axis_index("stack"), lax.axis_index("flow"), lax.axis_index("width")
    chip, core = me // 2, lax.rem(me, 2)
    other = 1 - core
    partner = {"stack": 2 * chip + other}
    f_next, f_prev = {"flow": lax.rem(fi + 1, nf)}, {"flow": lax.rem(fi + nf - 1, nf)}
    w_next, w_prev = {"width": lax.rem(wi + 1, nw)}, {"width": lax.rem(wi + nw - 1, nw)}

    def at_chip(steps):
        return {"stack": lax.rem(me + 2 * (steps % nch), ns)}

    part = nl // LOADS
    loads = [
        pltpu.make_async_copy(
            t_hbm.at[pl.ds(n * part, part)],
            tbuf.at[pl.ds(n * part, part), pl.ds(SUB, nr), :],
            t_sem.at[n],
        )
        for n in range(LOADS)
    ]
    small = [
        pltpu.make_async_copy(cat_hbm, cat_ref, t_sem.at[LOADS]),
        pltpu.make_async_copy(corr_hbm, corr_ref, t_sem.at[LOADS + 1]),
    ]
    for load in small + loads:
        load.start()

    blank = jnp.zeros((SUB, nc), jnp.float32)
    for j in range(nl):
        tbuf[j, 0:SUB, :] = blank
        tbuf[j, nr + SUB : nr + 2 * SUB, :] = blank

    barrier = pltpu.get_barrier_semaphore()
    near = (f_next, f_prev, w_next, w_prev, partner, at_chip(1), at_chip(-1))
    for dev in near:
        pl.semaphore_signal(barrier, inc=1, device_id=dev, device_id_type=MESH)

    def remote(src, dst, k, dev):
        return pltpu.make_async_remote_copy(
            src_ref=src,
            dst_ref=dst,
            send_sem=near_send.at[k],
            recv_sem=near_recv.at[k],
            device_id=dev,
            device_id_type=MESH,
        )

    def to_chip(src, dst, send, recv, k):
        return pltpu.make_async_remote_copy(
            src_ref=src,
            dst_ref=dst.at[chip],
            send_sem=send,
            recv_sem=recv,
            device_id={"stack": 2 * k + core},
            device_id_type=MESH,
        )

    for copy in small:
        copy.wait()
    layer = lax.broadcasted_iota(jnp.int32, (nl, nr), 0)
    column = lax.broadcasted_iota(jnp.int32, (nl, nr), 1)
    base = me * nl
    cats = [cat_ref[base + j] for j in range(nl)]
    catv = jnp.zeros((nl, nr), jnp.int32)
    for j in range(nl):
        catv = jnp.where(layer == j, cats[j], catv)
    kind = catv * 4 + corr_ref[...]
    k_own = pick_pair(kind, PLANE_K)
    film = pick_pair(kind, FILM)
    mass = 1.0 + film
    links = [link(scale, cats[j], cats[j + 1]) for j in range(nl - 1)]
    m = [mass[j : j + 1, :] for j in range(nl)]
    one, zero = jnp.ones((1, nr), jnp.float32), jnp.zeros((1, nr), jnp.float32)
    phi_ratio, psi_ratio = [None] * nl, [None] * nl
    up = m[nl - 2] + links[nl - 2]
    dn = m[1] + links[0]
    for j in range(nl - 2, 0, -1):
        inv = 1.0 / (up + links[j - 1])
        phi_ratio[j] = links[j - 1] * inv
        if j > 1:
            up = m[j - 1] + links[j - 1] * (up * inv)
        i = nl - 1 - j
        inv = 1.0 / (dn + links[i])
        psi_ratio[i] = links[i] * inv
        if i < nl - 2:
            dn = m[i + 1] + links[i] * (dn * inv)
    phi, psi = [one] + [None] * (nl - 2) + [zero], [zero] + [None] * (nl - 2) + [one]
    for j in range(1, nl - 1):
        phi[j] = phi[j - 1] * phi_ratio[j]
        i = nl - 1 - j
        psi[i] = psi[i + 1] * psi_ratio[i]
    gamma = links[0] * psi[1]
    g_a, g_b = m[0], m[nl - 1]
    for j in range(1, nl - 1):
        g_a = g_a + phi[j] * m[j]
        g_b = g_b + psi[j] * m[j]
    comp_tx[0:1, :] = g_a
    comp_tx[1:2, :] = g_b
    comp_tx[2:3, :] = gamma
    comp_tx[3:SUB, :] = jnp.zeros((SUB - 3, nr), jnp.float32)

    slot = lax.broadcasted_iota(jnp.int32, (SUB, LANES), 1)
    at_first, at_last = slot == 0, slot == LANES - 1
    height = lax.broadcasted_iota(jnp.int32, (SUB, LANES), 0)
    bottom, top = height == 0, height == SUB - 1
    span = LANES // PACK
    x0 = 5 * nl + 1
    u0 = 2 * nl + 1
    last, first = column == nr - 1, column == 0
    k_next = pltpu.roll(k_own, nr - 1, 1)
    c_lr = INPLANE * k_own
    for j in range(nl):
        cbuf[j : j + 1, :] = phi[j]
        cbuf[nl + j : nl + j + 1, :] = psi[j]
    cbuf[2 * nl + 1 : 3 * nl + 1, :] = INPLANE * face(k_own, k_next)
    cbuf[3 * nl + 1 : 4 * nl + 1, :] = c_lr
    cbuf[2 * nl : 2 * nl + 1, :] = 1.0 / gamma
    cbuf[4 * nl + 1 : LANES, :] = jnp.zeros((LANES - 4 * nl - 1, nr), jnp.float32)
    ct[...] = jnp.transpose(cbuf[...])

    def spread(first_q, last_q):
        tile = [ct[rows_of(rt), :] for rt in range(tiles)]
        for q in range(first_q, last_q):
            for rt in range(tiles):
                bc[q, rt] = lane(tile[rt], q)

    spread(0, 2 * nl + 1)

    for load in loads:
        load.wait()

    @pl.loop(0, tiles // PACK)
    def _(g):
        acc = [jnp.zeros((SUB, LANES), jnp.float32) for _ in range(2)]
        for side, (start, q) in enumerate(((0, 0), (nc - LANES, LANES - 1))):
            for s in range(PACK):
                r = rows_of(g * PACK + s + 1)
                for j in range(nl):
                    to = s * span + side * nl + j
                    value = pltpu.roll(tbuf[j, r, start : start + LANES], (to - q) % LANES, 1)
                    acc[side] = jnp.where(slot == to, value, acc[side])
        e_own[rows_of(g), :] = acc[0] + acc[1]

    pl.semaphore_wait(barrier, len(near))
    comp = remote(comp_tx, comp_rx, 6, partner)
    cor_dn = remote(corr_ref, corr_dn, 2, f_next)
    cor_up = remote(corr_ref, corr_up, 3, f_prev)
    row_dn = remote(t_hbm.at[:, pl.ds(nr - 1, 1), :], row_lo, 0, f_next)
    row_up = remote(t_hbm.at[:, pl.ds(0, 1), :], row_hi, 1, f_prev)
    for copy in (comp, cor_dn, cor_up, row_dn, row_up):
        copy.start()
    for steps in (1, -1):
        pl.semaphore_signal(ready.at[0], inc=1, device_id=at_chip(steps), device_id_type=MESH)

    edge_r = remote(e_own, e_left, 4, w_next)
    edge_l = remote(e_own, e_right, 5, w_prev)
    edge_r.start()
    edge_l.start()

    tile = [ct[rows_of(rt), :] for rt in range(tiles)]
    for j in range(nl):
        ups = [lane(tile[rt], u0 + j) for rt in range(tiles)]
        sides = [lane(tile[rt], u0 + nl + j) for rt in range(tiles)]
        for rt in range(tiles):
            if rt == tiles - 1:
                ups[rt] = jnp.where(top, 0.0, ups[rt])
            dn = pltpu.roll(jnp.where(top, ups[rt - 1] if rt > 0 else 0.0, ups[rt]), 1, 0)
            bc[u0 + j, rt] = ups[rt]
            bc[u0 + nl + j, rt] = sides[rt]
            bc[x0 + j, rt] = dn
            bc[x0 + nl + j, rt] = 1.0 - ((ups[rt] + dn) + 2.0 * sides[rt])
        kinds = [[FILM[c][n] * LEVEL[c] for c in range(3)] for n in range(4)]
        heat = [pick_scalar(cats[j], values) for values in kinds]
        cuts = [[INPLANE * 0.5 * (PLANE_K[c][n] + PLANE_K[c][n + 1]) for c in range(2)] for n in range(3)]
        cut = [pick_scalar(cats[j], values) for values in cuts]
        for rt in range(tiles):
            value = jnp.where(sides[rt] < cut[2], heat[2], heat[3])
            value = jnp.where(sides[rt] < cut[1], heat[1], value)
            bc[u0 + 2 * nl + j, rt] = jnp.where(sides[rt] < cut[0], heat[0], value)

    pl.semaphore_wait(ready.at[0], 2)
    if nch > 4:
        for steps in (2, -2):
            pl.semaphore_signal(ready.at[1], inc=1, device_id=at_chip(steps), device_id_type=MESH)

    columns = [slice(h * LANES, (h + 1) * LANES) for h in range(halves)]

    def right_side(rt):
        r0, r1, r2 = rows_of(rt), rows_of(rt + 1), rows_of(rt + 2)
        for j in range(nl):
            ts = [tbuf[j, r1, cols] for cols in columns]
            fwd = [pltpu.roll(t, 1, 1) for t in ts]
            bwd = [pltpu.roll(t, LANES - 1, 1) for t in ts]
            from_l = [0.0] + fwd[:-1]
            from_r = bwd[1:] + [0.0]
            for h, cols in enumerate(columns):
                t = ts[h]
                after = pltpu.roll(jnp.where(bottom, tbuf[j, r2, cols], t), SUB - 1, 0)
                before = pltpu.roll(jnp.where(top, tbuf[j, r0, cols], t), 1, 0)
                beside = jnp.where(at_first, from_l[h], fwd[h]) + jnp.where(at_last, from_r[h], bwd[h])
                rhs = bc[x0 + nl + j, rt] * t + bc[u0 + 2 * nl + j, rt]
                rhs = rhs + bc[u0 + j, rt] * after
                rhs = rhs + bc[x0 + j, rt] * before
                out_ref[j, r0, cols] = rhs + bc[u0 + nl + j, rt] * beside

    comp.wait_recv()
    theirs = [comp_rx[q : q + 1, :] for q in range(3)]
    low = [jnp.where(core == 0, a, b) for a, b in zip((g_a, g_b, gamma), theirs)]
    high = [jnp.where(core == 0, b, a) for a, b in zip((g_a, g_b, gamma), theirs)]
    mid = link(scale, cat_ref[2 * nl * chip + nl - 1], cat_ref[2 * nl * chip + nl])
    t_in = high[0] + high[2]
    t_inv = 1.0 / (t_in + mid)
    t_out = low[1] + mid * (t_in * t_inv)
    w_p = low[2] / (low[2] + t_out)
    w_q = w_p * (mid * t_inv)
    s_in = low[1] + low[2]
    s_inv = 1.0 / (s_in + mid)
    s_out = high[0] + mid * (s_in * s_inv)
    w_v = high[2] / (high[2] + s_out)
    w_u = w_v * (mid * s_inv)
    chip_gamma = low[2] * w_u
    chip_lo = low[0] + w_p * low[1] + w_q * high[0]
    chip_hi = high[1] + w_u * low[1] + w_v * high[0]
    merge = (w_p, w_q, w_u, w_v, w_u / chip_gamma, w_q / chip_gamma)
    for q, value in enumerate(merge + (chip_lo, chip_hi, chip_gamma)):
        cbuf[q : q + 1, :] = value
    ct[...] = jnp.transpose(cbuf[...])
    for k in range(nch):
        tile = ct[rows_of(2 * k + core), :]
        for q in range(len(merge)):
            mc[q, k] = lane(tile, q)

    @pl.loop(0, tiles // 2)
    def _(i):
        right_side(2 * i)
        right_side(2 * i + 1)

    if nch > 4:
        pl.semaphore_wait(ready.at[1], 2)

    @pl.loop(1, nch)
    def _(i):
        k = lax.rem(chip + i, nch)
        to_chip(ct.at[rows_of(2 * k + core), :], ct_rx, ct_send, ct_recv, k).start()

    ct_rx[chip] = ct[rows_of(me), :]

    cor_dn.wait_recv()
    cor_up.wait_recv()
    k_dn = pick_pair(catv * 4 + corr_dn[...], PLANE_K)
    k_up = pick_pair(catv * 4 + corr_up[...], PLANE_K)
    c_dn = INPLANE * face(k_own, pltpu.roll(k_dn, 1, 1))
    c_up = INPLANE * face(k_own, pltpu.roll(k_up, nr - 1, 1))
    c_dn = jnp.where(fi == 0, 0.0, jnp.broadcast_to(c_dn[:, 0:1], (nl, LANES)))
    c_up = jnp.where(fi == nf - 1, 0.0, jnp.broadcast_to(c_up[:, nr - 1 : nr], (nl, LANES)))
    row_dn.wait_recv()
    row_up.wait_recv()
    for j in range(nl):
        for cols in columns:
            for r, here, co, row in ((0, bottom, c_dn, row_lo), (nr - SUB, top, c_up, row_hi)):
                step = row[j, :, cols] - tbuf[j, r + SUB : r + 2 * SUB, cols]
                step = jnp.where(here, co[j : j + 1, :] * step, 0.0)
                out_ref[j, r : r + SUB, cols] = out_ref[j, r : r + SUB, cols] + step
    edge_r.wait_recv()
    edge_l.wait_recv()

    def block(rt):
        g, s = rt // PACK, lax.rem(rt, PACK)
        turn = lax.rem((PACK - s) * span, LANES)
        own = e_own[rows_of(g), :]
        left = jnp.where(wi > 0, e_left[rows_of(g), :], pltpu.roll(own, nl, 1))
        right = jnp.where(wi < nw - 1, e_right[rows_of(g), :], pltpu.roll(own, LANES - nl, 1))
        left, right = pltpu.roll(left, turn, 1), pltpu.roll(right, turn, 1)
        r0 = rows_of(rt)
        inv = bc[2 * nl, rt]
        pre, run = [None] * halves, [None] * halves
        ld_a, ld_b = [None] * halves, [None] * halves
        for j in range(nl):
            f, p, c_lr = bc[j, rt], bc[nl + j, rt], bc[u0 + nl + j, rt]
            for h, cols in enumerate(columns):
                rhs = out_ref[j, r0, cols]
                if h == 0:
                    edge = pltpu.roll(left, LANES - nl - j, 1)
                    rhs = rhs + jnp.where(at_first, c_lr * edge, 0.0)
                if h == halves - 1:
                    edge = pltpu.roll(right, LANES - 1 - j, 1)
                    rhs = rhs + jnp.where(at_last, c_lr * edge, 0.0)
                if j == 0:
                    ld_a[h] = rhs
                elif j == nl - 1:
                    ld_b[h] = pre[h] + rhs
                else:
                    if j == 1:
                        value = jnp.zeros((SUB, LANES), jnp.float32)
                        pre[h], run[h] = p * rhs, f * rhs
                    else:
                        value = (f * pre[h] - p * run[h]) * inv
                        pre[h], run[h] = pre[h] + p * rhs, run[h] + f * rhs
                    out_ref[j, r0, cols] = value
        for h in range(halves):
            ld_a[h] = ld_a[h] + run[h]
            fold[rt, :, h * LANES : (h + 1) * LANES] = run[h] * inv
        return ld_a, ld_b

    def to_partner(src, dst, send, recv, k):
        return pltpu.make_async_remote_copy(
            src_ref=src.at[k],
            dst_ref=dst.at[k],
            send_sem=send,
            recv_sem=recv.at[k],
            device_id=partner,
            device_id_type=MESH,
        )

    def whole(ref, send, recv):
        return pltpu.make_async_remote_copy(
            src_ref=ref,
            dst_ref=ref,
            send_sem=send,
            recv_sem=recv,
            device_id=partner,
            device_id_type=MESH,
        )

    def inward(t):
        return [lax.rem(chip + nch - half + t, nch), lax.rem(chip + half - 1 - t, nch)]

    def outward(t):
        return [lax.rem(chip + t, nch), lax.rem(chip + nch - 1 - t, nch)]

    def for_partner(t):
        ks = inward(t)
        found = [block(2 * k + other) for k in ks]
        for k, (ld_a, ld_b) in zip(ks, found):
            for h, cols in enumerate(columns):
                pair_tx[k, 0, :, cols] = ld_a[h]
                pair_tx[k, 1, :, cols] = ld_b[h]
            to_partner(pair_tx, pair_rx, pair_send, pair_recv, k).start()

    def for_chip(t):
        ks = inward(t)
        found = [block(2 * k + core) for k in ks]
        for k, (ld_a, ld_b) in zip(ks, found):
            to_partner(pair_tx, pair_rx, pair_send, pair_recv, k).wait_recv()
            p, q, u, v = (mc[n, k] for n in range(4))
            for h, cols in enumerate(columns):
                their_a, their_b = pair_rx[k, 0, :, cols], pair_rx[k, 1, :, cols]
                f_b = jnp.where(core == 0, ld_b[h], their_b)
                f_a = jnp.where(core == 0, their_a, ld_a[h])
                f_lo = jnp.where(core == 0, ld_a[h], their_a)
                f_hi = jnp.where(core == 0, their_b, ld_b[h])
                to_lo = p * f_b + q * f_a
                to_hi = u * f_b + v * f_a
                inner[k, 0, :, cols] = to_lo
                inner[k, 1, :, cols] = to_hi
                ld_tx[k, 0, :, cols] = f_lo + to_lo
                ld_tx[k, 1, :, cols] = f_hi + to_hi

            @pl.when(k != chip)
            def _():
                to_chip(ld_tx.at[k], ld_rx, ld_send, ld_recv, k).start()

    lag = min(2, half)
    for t in range(lag):
        for_partner(t)

    @pl.loop(lag, half)
    def _(t):
        for_partner(t)
        for_chip(t - lag)

    @pl.loop(half - lag, half)
    def _(t):
        for_chip(t)

    ld_rx[chip] = ld_tx[chip]

    others = pl.ds(0, nch - 1)
    whole(ct_rx.at[others], ct_send, ct_recv).wait_recv()
    s, hold = None, None
    for d in range(nch):
        g_lo, g_hi, gam = (lane(ct_rx[d], len(merge) + q) for q in range(3))
        s = g_lo if d == 0 else g_lo + hold * s
        inv = 1.0 / (s + gam)
        hold = gam * inv
        piv[2 * d, 0], piv[2 * d, 1] = inv, hold
        s = g_hi + hold * s
        if d < nch - 1:
            outer = link(scale, cat_ref[2 * nl * (d + 1) - 1], cat_ref[2 * nl * (d + 1)])
            inv = 1.0 / (s + outer)
            hold = outer * inv
        else:
            inv = 1.0 / s
            hold = jnp.zeros_like(inv)
        piv[2 * d + 1, 0], piv[2 * d + 1, 1] = inv, hold

    whole(ld_rx.at[others], ld_send, ld_recv).wait_recv()
    for cols in columns:
        flow = []
        for n in range(2 * nch):
            now = ld_rx[n // 2, n % 2, :, cols]
            if n > 0:
                now = now + piv[n - 1, 1] * flow[n - 1]
            flow.append(now)
        x = flow[-1] * piv[2 * nch - 1, 0]
        sol_tx[nch - 1, 1, :, cols] = x
        for n in range(2 * nch - 2, -1, -1):
            x = flow[n] * piv[n, 0] + piv[n, 1] * x
            sol_tx[n // 2, n % 2, :, cols] = x

    @pl.loop(0, nch - 1)
    def _(i):
        steps = (half - (i + 1) // 2) * (1 - 2 * lax.rem(i, 2))
        k = lax.rem(chip + nch + steps, nch)
        to_chip(sol_tx.at[k], sol_rx, sol_send, sol_recv.at[chip], k).start()

    sol_rx[chip] = sol_tx[chip]

    def finish(rt, lo, hi):
        r = rows_of(rt)
        for h, cols in enumerate(columns):
            out_ref[0, r, cols] = lo[h]
            out_ref[nl - 1, r, cols] = hi[h]
            bent = hi[h] + fold[rt, :, cols]
            for j in range(1, nl - 1):
                ends = bc[j, rt] * lo[h] + bc[nl + j, rt] * bent
                out_ref[j, r, cols] = out_ref[j, r, cols] + ends

    def finish_own(t):
        ks = outward(t)
        found = []
        for k in ks:

            @pl.when(k != chip)
            def _():
                to_chip(sol_tx.at[k], sol_rx, sol_send, sol_recv.at[k], k).wait_recv()

            p, q, u, v, s_b, s_a = (mc[n, k] for n in range(6))
            lo, hi = [None] * halves, [None] * halves
            for h, cols in enumerate(columns):
                x_lo, x_hi = sol_rx[k, 0, :, cols], sol_rx[k, 1, :, cols]
                x_b = p * x_lo + u * x_hi + s_b * inner[k, 0, :, cols]
                x_a = q * x_lo + v * x_hi + s_a * inner[k, 1, :, cols]
                lo[h] = jnp.where(core == 0, x_lo, x_a)
                hi[h] = jnp.where(core == 0, x_b, x_hi)
                end_tx[k, 0, :, cols] = jnp.where(core == 0, x_a, x_lo)
                end_tx[k, 1, :, cols] = jnp.where(core == 0, x_hi, x_b)
            to_partner(end_tx, ends_buf, end_send, end_recv, k).start()
            found.append((lo, hi))
        for k, (lo, hi) in zip(ks, found):
            finish(2 * k + core, lo, hi)

    def finish_theirs(t):
        ks = outward(t)
        for k in ks:
            to_partner(end_tx, ends_buf, end_send, end_recv, k).wait_recv()
        for k in ks:
            lo = [ends_buf[k, 0, :, cols] for cols in columns]
            hi = [ends_buf[k, 1, :, cols] for cols in columns]
            finish(2 * k + other, lo, hi)

    @pl.loop(0, half)
    def _(t):
        finish_own(t)

    @pl.loop(0, half)
    def _(t):
        finish_theirs(t)

    for copy in (comp, row_dn, row_up, cor_dn, cor_up, edge_r, edge_l):
        copy.wait_send()
    whole(pair_tx, pair_send, ct_recv).wait_send()
    whole(end_tx, end_send, ct_recv).wait_send()
    whole(ct_rx.at[others], ct_send, ct_recv).wait_send()
    whole(ld_tx.at[others], ld_send, ct_recv).wait_send()
    whole(sol_tx.at[others], sol_send, ct_recv).wait_send()


def copy_out(parts, x_ref, out_ref, sem):
    step = x_ref.shape[0] // parts
    copies = [
        pltpu.make_async_copy(
            x_ref.at[pl.ds(n * step, step)], out_ref.at[pl.ds(n * step, step)], sem.at[n]
        )
        for n in range(parts)
    ]
    for copy in copies:
        copy.start()
    for copy in copies:
        copy.wait()


def per_device(initial_thermal_state, plate_fluid_category, corrugation_type_grid):
    nl, nr, nc = initial_thermal_state.shape
    ns, nf, nw = lax.axis_size("stack"), lax.axis_size("flow"), lax.axis_size("width")
    nch, tiles = ns // 2, nr // SUB
    total = nl * ns
    scale = STACK_SCALE * float(total * total)
    dims = (ns, nf, nw, nl, nr, nc, scale)
    f32 = jnp.float32
    packed = (tiles // PACK * SUB, LANES)
    tile_pair = pltpu.VMEM((nch, 2, SUB, nc), f32)
    dma = pltpu.SemaphoreType.DMA
    result = pl.pallas_call(
        functools.partial(kernel, dims),
        out_shape=pltpu.VMEM((nl, nr, nc), f32),
        in_specs=[
            pl.BlockSpec(memory_space=pl.ANY),
            pl.BlockSpec(memory_space=pl.ANY),
            pl.BlockSpec(memory_space=pl.ANY),
        ],
        out_specs=pl.BlockSpec(memory_space=pltpu.VMEM),
        scratch_shapes=[
            pltpu.SMEM((total,), jnp.int32),
            pltpu.VMEM((nl, nr), jnp.int32),
            pltpu.VMEM((nl, nr + 2 * SUB, nc), f32),
            pltpu.VMEM((nl, 1, nc), f32),
            pltpu.VMEM((nl, 1, nc), f32),
            pltpu.VMEM(packed, f32),
            pltpu.VMEM(packed, f32),
            pltpu.VMEM(packed, f32),
            pltpu.VMEM((nl, nr), jnp.int32),
            pltpu.VMEM((nl, nr), jnp.int32),
            pltpu.VMEM((SUB, nr), f32),
            pltpu.VMEM((SUB, nr), f32),
            pltpu.VMEM((LANES, nr), f32),
            pltpu.VMEM((nr, LANES), f32),
            pltpu.VMEM((nch, SUB, LANES), f32),
            pltpu.VMEM((7 * nl + 1, tiles, SUB, LANES), f32),
            pltpu.VMEM((6, nch, SUB, LANES), f32),
            pltpu.VMEM((tiles, SUB, nc), f32),
        ]
        + [tile_pair] * 9
        + [
            pltpu.VMEM((2 * nch, 2, SUB, LANES), f32),
            dma((LOADS + 2,)),
            dma((7,)),
            dma((7,)),
            dma,
            dma,
            dma,
            dma((nch,)),
            dma,
            dma,
            dma,
            dma((nch,)),
            dma,
            dma((nch,)),
        ]
        + [pltpu.SemaphoreType.REGULAR((2,))],
        compiler_params=pltpu.CompilerParams(
            collective_id=0,
            has_side_effects=True,
            vmem_limit_bytes=VMEM_BYTES - 4 * nl * nr * nc - (1 << 20),
        ),
        name="stack_step",
    )(plate_fluid_category, corrugation_type_grid, initial_thermal_state)
    parts = 4
    return pl.pallas_call(
        functools.partial(copy_out, parts),
        out_shape=jax.ShapeDtypeStruct((nl, nr, nc), f32),
        in_specs=[pl.BlockSpec(memory_space=pltpu.VMEM)],
        out_specs=pl.BlockSpec(memory_space=pl.ANY),
        scratch_shapes=[dma((parts,))],
        compiler_params=pltpu.CompilerParams(vmem_limit_bytes=1 << 20),
        name="copy_out",
    )(result)


def solution(mesh):
    placed = (P("stack", "flow", "width"), P(), P("stack", "flow"))
    return jax.shard_map(
        per_device,
        mesh=mesh,
        in_specs=placed,
        out_specs=P("stack", "flow", "width"),
        check_vma=False,
    )
```

```python
import functools

import jax
import jax.numpy as jnp
from jax import lax
from jax.experimental import pallas as pl
from jax.experimental.pallas import tpu as pltpu
from jax.sharding import PartitionSpec as P

STACK_K = (0.15, 0.25, 1.0)
PLANE_K = ((0.35, 0.5, 0.7, 0.9), (0.3, 0.45, 0.65, 0.85), (0.8, 0.9, 1.0, 0.95))
FILM = ((0.4, 0.8, 1.2, 1.6), (0.3, 0.6, 1.0, 1.4), (0.0, 0.0, 0.0, 0.0))
LEVEL = (1.5, -1.0, 0.0)
INPLANE = 0.24
STACK_SCALE = 0.2
MESH = pl.DeviceIdType.MESH
SUB = 8
LANES = 128
PACK = 4
VMEM_BYTES = 67043328
LOADS = 4


def face(a, b):
    return 2.0 * a * b / (a + b)


def pick_scalar(code, values):
    out = jnp.float32(values[-1])
    for i in range(len(values) - 2, -1, -1):
        out = jnp.where(code == i, jnp.float32(values[i]), out)
    return out


def pick_pair(index, table):
    flat = [v for row in table for v in row]
    out = jnp.full(index.shape, flat[-1], jnp.float32)
    for i in range(len(flat) - 2, -1, -1):
        if flat[i] != flat[-1]:
            out = jnp.where(index == i, jnp.float32(flat[i]), out)
    return out


def link(scale, first, second):
    rows = []
    for a in STACK_K:
        rows.append(pick_scalar(second, [scale * face(a, b) for b in STACK_K]))
    return jnp.where(first == 0, rows[0], jnp.where(first == 1, rows[1], rows[2]))


def lane(tile, q):
    return jnp.broadcast_to(tile[:, q : q + 1], (tile.shape[0], LANES))


def rows_of(tile):
    return pl.ds(pl.multiple_of(tile * SUB, SUB), SUB)


def kernel(
    dims,
    cat_hbm,
    corr_hbm,
    t_hbm,
    out_ref,
    cat_ref,
    corr_ref,
    tbuf,
    row_lo,
    row_hi,
    e_own,
    e_left,
    e_right,
    corr_dn,
    corr_up,
    comp_tx,
    comp_rx,
    cbuf,
    ct,
    ct_rx,
    bc,
    mc,
    fold,
    pair_tx,
    pair_rx,
    inner,
    ld_tx,
    ld_rx,
    sol_tx,
    sol_rx,
    end_tx,
    ends_buf,
    piv,
    t_sem,
    near_send,
    near_recv,
    ct_send,
    ct_recv,
    pair_send,
    pair_recv,
    ld_send,
    ld_recv,
    sol_send,
    sol_recv,
    end_send,
    end_recv,
    ready,
):
    ns, nf, nw, nl, nr, nc, scale = dims
    nch, tiles, halves = ns // 2, nr // SUB, nc // LANES
    half = nch // 2
    me, fi, wi = lax.axis_index("stack"), lax.axis_index("flow"), lax.axis_index("width")
    chip, core = me // 2, lax.rem(me, 2)
    other = 1 - core
    partner = {"stack": 2 * chip + other}
    f_next, f_prev = {"flow": lax.rem(fi + 1, nf)}, {"flow": lax.rem(fi + nf - 1, nf)}
    w_next, w_prev = {"width": lax.rem(wi + 1, nw)}, {"width": lax.rem(wi + nw - 1, nw)}

    def at_chip(steps):
        return {"stack": lax.rem(me + 2 * (steps % nch), ns)}

    part = nl // LOADS
    loads = [
        pltpu.make_async_copy(
            t_hbm.at[pl.ds(n * part, part)],
            tbuf.at[pl.ds(n * part, part), pl.ds(SUB, nr), :],
            t_sem.at[n],
        )
        for n in range(LOADS)
    ]
    small = [
        pltpu.make_async_copy(cat_hbm, cat_ref, t_sem.at[LOADS]),
        pltpu.make_async_copy(corr_hbm, corr_ref, t_sem.at[LOADS + 1]),
    ]
    for load in small + loads:
        load.start()

    blank = jnp.zeros((SUB, nc), jnp.float32)
    for j in range(nl):
        tbuf[j, 0:SUB, :] = blank
        tbuf[j, nr + SUB : nr + 2 * SUB, :] = blank

    barrier = pltpu.get_barrier_semaphore()
    near = (f_next, f_prev, w_next, w_prev, partner, at_chip(1), at_chip(-1))
    for dev in near:
        pl.semaphore_signal(barrier, inc=1, device_id=dev, device_id_type=MESH)

    def remote(src, dst, k, dev):
        return pltpu.make_async_remote_copy(
            src_ref=src,
            dst_ref=dst,
            send_sem=near_send.at[k],
            recv_sem=near_recv.at[k],
            device_id=dev,
            device_id_type=MESH,
        )

    def to_chip(src, dst, send, recv, k):
        return pltpu.make_async_remote_copy(
            src_ref=src,
            dst_ref=dst.at[chip],
            send_sem=send,
            recv_sem=recv,
            device_id={"stack": 2 * k + core},
            device_id_type=MESH,
        )

    for copy in small:
        copy.wait()
    layer = lax.broadcasted_iota(jnp.int32, (nl, nr), 0)
    column = lax.broadcasted_iota(jnp.int32, (nl, nr), 1)
    base = me * nl
    cats = [cat_ref[base + j] for j in range(nl)]
    catv = jnp.zeros((nl, nr), jnp.int32)
    for j in range(nl):
        catv = jnp.where(layer == j, cats[j], catv)
    kind = catv * 4 + corr_ref[...]
    k_own = pick_pair(kind, PLANE_K)
    film = pick_pair(kind, FILM)
    mass = 1.0 + film
    links = [link(scale, cats[j], cats[j + 1]) for j in range(nl - 1)]
    m = [mass[j : j + 1, :] for j in range(nl)]
    one, zero = jnp.ones((1, nr), jnp.float32), jnp.zeros((1, nr), jnp.float32)
    phi_ratio, psi_ratio = [None] * nl, [None] * nl
    up = m[nl - 2] + links[nl - 2]
    dn = m[1] + links[0]
    for j in range(nl - 2, 0, -1):
        inv = 1.0 / (up + links[j - 1])
        phi_ratio[j] = links[j - 1] * inv
        if j > 1:
            up = m[j - 1] + links[j - 1] * (up * inv)
        i = nl - 1 - j
        inv = 1.0 / (dn + links[i])
        psi_ratio[i] = links[i] * inv
        if i < nl - 2:
            dn = m[i + 1] + links[i] * (dn * inv)
    phi, psi = [one] + [None] * (nl - 2) + [zero], [zero] + [None] * (nl - 2) + [one]
    for j in range(1, nl - 1):
        phi[j] = phi[j - 1] * phi_ratio[j]
        i = nl - 1 - j
        psi[i] = psi[i + 1] * psi_ratio[i]
    gamma = links[0] * psi[1]
    g_a, g_b = m[0], m[nl - 1]
    for j in range(1, nl - 1):
        g_a = g_a + phi[j] * m[j]
        g_b = g_b + psi[j] * m[j]
    comp_tx[0:1, :] = g_a
    comp_tx[1:2, :] = g_b
    comp_tx[2:3, :] = gamma
    comp_tx[3:SUB, :] = jnp.zeros((SUB - 3, nr), jnp.float32)

    slot = lax.broadcasted_iota(jnp.int32, (SUB, LANES), 1)
    at_first, at_last = slot == 0, slot == LANES - 1
    height = lax.broadcasted_iota(jnp.int32, (SUB, LANES), 0)
    bottom, top = height == 0, height == SUB - 1
    span = LANES // PACK
    x0 = 5 * nl + 1
    u0 = 2 * nl + 1
    last, first = column == nr - 1, column == 0
    k_next = pltpu.roll(k_own, nr - 1, 1)
    c_lr = INPLANE * k_own
    for j in range(nl):
        cbuf[j : j + 1, :] = phi[j]
        cbuf[nl + j : nl + j + 1, :] = psi[j]
    cbuf[2 * nl + 1 : 3 * nl + 1, :] = INPLANE * face(k_own, k_next)
    cbuf[3 * nl + 1 : 4 * nl + 1, :] = c_lr
    cbuf[2 * nl : 2 * nl + 1, :] = 1.0 / gamma
    cbuf[4 * nl + 1 : LANES, :] = jnp.zeros((LANES - 4 * nl - 1, nr), jnp.float32)
    ct[...] = jnp.transpose(cbuf[...])

    def spread(first_q, last_q):
        tile = [ct[rows_of(rt), :] for rt in range(tiles)]
        for q in range(first_q, last_q):
            for rt in range(tiles):
                bc[q, rt] = lane(tile[rt], q)

    spread(0, 2 * nl + 1)

    for load in loads:
        load.wait()

    @pl.loop(0, tiles // PACK)
    def _(g):
        acc = [jnp.zeros((SUB, LANES), jnp.float32) for _ in range(2)]
        for side, (start, q) in enumerate(((0, 0), (nc - LANES, LANES - 1))):
            for s in range(PACK):
                r = rows_of(g * PACK + s + 1)
                for j in range(nl):
                    to = s * span + side * nl + j
                    value = pltpu.roll(tbuf[j, r, start : start + LANES], (to - q) % LANES, 1)
                    acc[side] = jnp.where(slot == to, value, acc[side])
        e_own[rows_of(g), :] = acc[0] + acc[1]

    pl.semaphore_wait(barrier, len(near))
    comp = remote(comp_tx, comp_rx, 6, partner)
    cor_dn = remote(corr_ref, corr_dn, 2, f_next)
    cor_up = remote(corr_ref, corr_up, 3, f_prev)
    row_dn = remote(t_hbm.at[:, pl.ds(nr - 1, 1), :], row_lo, 0, f_next)
    row_up = remote(t_hbm.at[:, pl.ds(0, 1), :], row_hi, 1, f_prev)
    for copy in (comp, cor_dn, cor_up, row_dn, row_up):
        copy.start()
    for steps in (1, -1):
        pl.semaphore_signal(ready.at[0], inc=1, device_id=at_chip(steps), device_id_type=MESH)

    edge_r = remote(e_own, e_left, 4, w_next)
    edge_l = remote(e_own, e_right, 5, w_prev)
    edge_r.start()
    edge_l.start()

    tile = [ct[rows_of(rt), :] for rt in range(tiles)]
    for j in range(nl):
        ups = [lane(tile[rt], u0 + j) for rt in range(tiles)]
        sides = [lane(tile[rt], u0 + nl + j) for rt in range(tiles)]
        for rt in range(tiles):
            if rt == tiles - 1:
                ups[rt] = jnp.where(top, 0.0, ups[rt])
            dn = pltpu.roll(jnp.where(top, ups[rt - 1] if rt > 0 else 0.0, ups[rt]), 1, 0)
            bc[u0 + j, rt] = ups[rt]
            bc[u0 + nl + j, rt] = sides[rt]
            bc[x0 + j, rt] = dn
            bc[x0 + nl + j, rt] = 1.0 - ((ups[rt] + dn) + 2.0 * sides[rt])
        kinds = [[FILM[c][n] * LEVEL[c] for c in range(3)] for n in range(4)]
        heat = [pick_scalar(cats[j], values) for values in kinds]
        cuts = [[INPLANE * 0.5 * (PLANE_K[c][n] + PLANE_K[c][n + 1]) for c in range(2)] for n in range(3)]
        cut = [pick_scalar(cats[j], values) for values in cuts]
        for rt in range(tiles):
            value = jnp.where(sides[rt] < cut[2], heat[2], heat[3])
            value = jnp.where(sides[rt] < cut[1], heat[1], value)
            bc[u0 + 2 * nl + j, rt] = jnp.where(sides[rt] < cut[0], heat[0], value)

    pl.semaphore_wait(ready.at[0], 2)
    if nch > 4:
        for steps in (2, -2):
            pl.semaphore_signal(ready.at[1], inc=1, device_id=at_chip(steps), device_id_type=MESH)

    columns = [slice(h * LANES, (h + 1) * LANES) for h in range(halves)]

    def right_side(rt):
        r0, r1, r2 = rows_of(rt), rows_of(rt + 1), rows_of(rt + 2)
        for j in range(nl):
            ts = [tbuf[j, r1, cols] for cols in columns]
            fwd = [pltpu.roll(t, 1, 1) for t in ts]
            bwd = [pltpu.roll(t, LANES - 1, 1) for t in ts]
            from_l = [0.0] + fwd[:-1]
            from_r = bwd[1:] + [0.0]
            for h, cols in enumerate(columns):
                t = ts[h]
                after = pltpu.roll(jnp.where(bottom, tbuf[j, r2, cols], t), SUB - 1, 0)
                before = pltpu.roll(jnp.where(top, tbuf[j, r0, cols], t), 1, 0)
                beside = jnp.where(at_first, from_l[h], fwd[h]) + jnp.where(at_last, from_r[h], bwd[h])
                rhs = bc[x0 + nl + j, rt] * t + bc[u0 + 2 * nl + j, rt]
                rhs = rhs + bc[u0 + j, rt] * after
                rhs = rhs + bc[x0 + j, rt] * before
                out_ref[j, r0, cols] = rhs + bc[u0 + nl + j, rt] * beside

    comp.wait_recv()
    theirs = [comp_rx[q : q + 1, :] for q in range(3)]
    low = [jnp.where(core == 0, a, b) for a, b in zip((g_a, g_b, gamma), theirs)]
    high = [jnp.where(core == 0, b, a) for a, b in zip((g_a, g_b, gamma), theirs)]
    mid = link(scale, cat_ref[2 * nl * chip + nl - 1], cat_ref[2 * nl * chip + nl])
    t_in = high[0] + high[2]
    t_inv = 1.0 / (t_in + mid)
    t_out = low[1] + mid * (t_in * t_inv)
    w_p = low[2] / (low[2] + t_out)
    w_q = w_p * (mid * t_inv)
    s_in = low[1] + low[2]
    s_inv = 1.0 / (s_in + mid)
    s_out = high[0] + mid * (s_in * s_inv)
    w_v = high[2] / (high[2] + s_out)
    w_u = w_v * (mid * s_inv)
    chip_gamma = low[2] * w_u
    chip_lo = low[0] + w_p * low[1] + w_q * high[0]
    chip_hi = high[1] + w_u * low[1] + w_v * high[0]
    merge = (w_p, w_q, w_u, w_v, w_u / chip_gamma, w_q / chip_gamma)
    for q, value in enumerate(merge + (chip_lo, chip_hi, chip_gamma)):
        cbuf[q : q + 1, :] = value
    ct[...] = jnp.transpose(cbuf[...])
    for k in range(nch):
        tile = ct[rows_of(2 * k + core), :]
        for q in range(len(merge)):
            mc[q, k] = lane(tile, q)

    @pl.loop(0, tiles // PACK)
    def _(i):
        for n in range(PACK):
            right_side(PACK * i + n)

    if nch > 4:
        pl.semaphore_wait(ready.at[1], 2)

    @pl.loop(1, nch)
    def _(i):
        k = lax.rem(chip + i, nch)
        to_chip(ct.at[rows_of(2 * k + core), :], ct_rx, ct_send, ct_recv, k).start()

    ct_rx[chip] = ct[rows_of(me), :]

    cor_dn.wait_recv()
    cor_up.wait_recv()
    k_dn = pick_pair(catv * 4 + corr_dn[...], PLANE_K)
    k_up = pick_pair(catv * 4 + corr_up[...], PLANE_K)
    c_dn = INPLANE * face(k_own, pltpu.roll(k_dn, 1, 1))
    c_up = INPLANE * face(k_own, pltpu.roll(k_up, nr - 1, 1))
    c_dn = jnp.where(fi == 0, 0.0, jnp.broadcast_to(c_dn[:, 0:1], (nl, LANES)))
    c_up = jnp.where(fi == nf - 1, 0.0, jnp.broadcast_to(c_up[:, nr - 1 : nr], (nl, LANES)))
    row_dn.wait_recv()
    row_up.wait_recv()
    for j in range(nl):
        for cols in columns:
            for r, here, co, row in ((0, bottom, c_dn, row_lo), (nr - SUB, top, c_up, row_hi)):
                step = row[j, :, cols] - tbuf[j, r + SUB : r + 2 * SUB, cols]
                step = jnp.where(here, co[j : j + 1, :] * step, 0.0)
                out_ref[j, r : r + SUB, cols] = out_ref[j, r : r + SUB, cols] + step
    edge_r.wait_recv()
    edge_l.wait_recv()

    def block(rt):
        g, s = rt // PACK, lax.rem(rt, PACK)
        turn = lax.rem((PACK - s) * span, LANES)
        own = e_own[rows_of(g), :]
        left = jnp.where(wi > 0, e_left[rows_of(g), :], pltpu.roll(own, nl, 1))
        right = jnp.where(wi < nw - 1, e_right[rows_of(g), :], pltpu.roll(own, LANES - nl, 1))
        left, right = pltpu.roll(left, turn, 1), pltpu.roll(right, turn, 1)
        r0 = rows_of(rt)
        inv = bc[2 * nl, rt]
        pre, run = [None] * halves, [None] * halves
        ld_a, ld_b = [None] * halves, [None] * halves
        for j in range(nl):
            f, p, c_lr = bc[j, rt], bc[nl + j, rt], bc[u0 + nl + j, rt]
            for h, cols in enumerate(columns):
                rhs = out_ref[j, r0, cols]
                if h == 0:
                    edge = pltpu.roll(left, LANES - nl - j, 1)
                    rhs = rhs + jnp.where(at_first, c_lr * edge, 0.0)
                if h == halves - 1:
                    edge = pltpu.roll(right, LANES - 1 - j, 1)
                    rhs = rhs + jnp.where(at_last, c_lr * edge, 0.0)
                if j == 0:
                    ld_a[h] = rhs
                elif j == nl - 1:
                    ld_b[h] = pre[h] + rhs
                else:
                    if j == 1:
                        value = jnp.zeros((SUB, LANES), jnp.float32)
                        pre[h], run[h] = p * rhs, f * rhs
                    else:
                        value = (f * pre[h] - p * run[h]) * inv
                        pre[h], run[h] = pre[h] + p * rhs, run[h] + f * rhs
                    out_ref[j, r0, cols] = value
        for h in range(halves):
            ld_a[h] = ld_a[h] + run[h]
            fold[rt, :, h * LANES : (h + 1) * LANES] = run[h] * inv
        return ld_a, ld_b

    def to_partner(src, dst, send, recv, k):
        return pltpu.make_async_remote_copy(
            src_ref=src.at[k],
            dst_ref=dst.at[k],
            send_sem=send,
            recv_sem=recv.at[k],
            device_id=partner,
            device_id_type=MESH,
        )

    def whole(ref, send, recv):
        return pltpu.make_async_remote_copy(
            src_ref=ref,
            dst_ref=ref,
            send_sem=send,
            recv_sem=recv,
            device_id=partner,
            device_id_type=MESH,
        )

    def inward(t):
        return [lax.rem(chip + nch - half + t, nch), lax.rem(chip + half - 1 - t, nch)]

    def outward(t):
        return [lax.rem(chip + t, nch), lax.rem(chip + nch - 1 - t, nch)]

    def for_partner(t):
        ks = inward(t)
        found = [block(2 * k + other) for k in ks]
        for k, (ld_a, ld_b) in zip(ks, found):
            for h, cols in enumerate(columns):
                pair_tx[k, 0, :, cols] = ld_a[h]
                pair_tx[k, 1, :, cols] = ld_b[h]
            to_partner(pair_tx, pair_rx, pair_send, pair_recv, k).start()

    def for_chip(t):
        ks = inward(t)
        found = [block(2 * k + core) for k in ks]
        for k, (ld_a, ld_b) in zip(ks, found):
            to_partner(pair_tx, pair_rx, pair_send, pair_recv, k).wait_recv()
            p, q, u, v = (mc[n, k] for n in range(4))
            for h, cols in enumerate(columns):
                their_a, their_b = pair_rx[k, 0, :, cols], pair_rx[k, 1, :, cols]
                f_b = jnp.where(core == 0, ld_b[h], their_b)
                f_a = jnp.where(core == 0, their_a, ld_a[h])
                f_lo = jnp.where(core == 0, ld_a[h], their_a)
                f_hi = jnp.where(core == 0, their_b, ld_b[h])
                to_lo = p * f_b + q * f_a
                to_hi = u * f_b + v * f_a
                inner[k, 0, :, cols] = to_lo
                inner[k, 1, :, cols] = to_hi
                ld_tx[k, 0, :, cols] = f_lo + to_lo
                ld_tx[k, 1, :, cols] = f_hi + to_hi

            @pl.when(k != chip)
            def _():
                to_chip(ld_tx.at[k], ld_rx, ld_send, ld_recv, k).start()

    lag = min(2, half)
    for t in range(lag):
        for_partner(t)

    @pl.loop(lag, half)
    def _(t):
        for_partner(t)
        for_chip(t - lag)

    @pl.loop(half - lag, half)
    def _(t):
        for_chip(t)

    ld_rx[chip] = ld_tx[chip]

    others = pl.ds(0, nch - 1)
    whole(ct_rx.at[others], ct_send, ct_recv).wait_recv()
    s, hold = None, None
    for d in range(nch):
        g_lo, g_hi, gam = (lane(ct_rx[d], len(merge) + q) for q in range(3))
        s = g_lo if d == 0 else g_lo + hold * s
        inv = 1.0 / (s + gam)
        hold = gam * inv
        piv[2 * d, 0], piv[2 * d, 1] = inv, hold
        s = g_hi + hold * s
        if d < nch - 1:
            outer = link(scale, cat_ref[2 * nl * (d + 1) - 1], cat_ref[2 * nl * (d + 1)])
            inv = 1.0 / (s + outer)
            hold = outer * inv
        else:
            inv = 1.0 / s
            hold = jnp.zeros_like(inv)
        piv[2 * d + 1, 0], piv[2 * d + 1, 1] = inv, hold

    whole(ld_rx.at[others], ld_send, ld_recv).wait_recv()
    for cols in columns:
        flow = []
        for n in range(2 * nch):
            now = ld_rx[n // 2, n % 2, :, cols]
            if n > 0:
                now = now + piv[n - 1, 1] * flow[n - 1]
            flow.append(now)
        x = flow[-1] * piv[2 * nch - 1, 0]
        sol_tx[nch - 1, 1, :, cols] = x
        for n in range(2 * nch - 2, -1, -1):
            x = flow[n] * piv[n, 0] + piv[n, 1] * x
            sol_tx[n // 2, n % 2, :, cols] = x

    @pl.loop(0, nch - 1)
    def _(i):
        steps = (half - (i + 1) // 2) * (1 - 2 * lax.rem(i, 2))
        k = lax.rem(chip + nch + steps, nch)
        to_chip(sol_tx.at[k], sol_rx, sol_send, sol_recv.at[chip], k).start()

    sol_rx[chip] = sol_tx[chip]

    def finish(rt, lo, hi):
        r = rows_of(rt)
        for h, cols in enumerate(columns):
            out_ref[0, r, cols] = lo[h]
            out_ref[nl - 1, r, cols] = hi[h]
            bent = hi[h] + fold[rt, :, cols]
            for j in range(1, nl - 1):
                ends = bc[j, rt] * lo[h] + bc[nl + j, rt] * bent
                out_ref[j, r, cols] = out_ref[j, r, cols] + ends

    def finish_own(t):
        ks = outward(t)
        found = []
        for k in ks:

            @pl.when(k != chip)
            def _():
                to_chip(sol_tx.at[k], sol_rx, sol_send, sol_recv.at[k], k).wait_recv()

            p, q, u, v, s_b, s_a = (mc[n, k] for n in range(6))
            lo, hi = [None] * halves, [None] * halves
            for h, cols in enumerate(columns):
                x_lo, x_hi = sol_rx[k, 0, :, cols], sol_rx[k, 1, :, cols]
                x_b = p * x_lo + u * x_hi + s_b * inner[k, 0, :, cols]
                x_a = q * x_lo + v * x_hi + s_a * inner[k, 1, :, cols]
                lo[h] = jnp.where(core == 0, x_lo, x_a)
                hi[h] = jnp.where(core == 0, x_b, x_hi)
                end_tx[k, 0, :, cols] = jnp.where(core == 0, x_a, x_lo)
                end_tx[k, 1, :, cols] = jnp.where(core == 0, x_hi, x_b)
            to_partner(end_tx, ends_buf, end_send, end_recv, k).start()
            found.append((lo, hi))
        for k, (lo, hi) in zip(ks, found):
            finish(2 * k + core, lo, hi)

    def finish_theirs(t):
        ks = outward(t)
        for k in ks:
            to_partner(end_tx, ends_buf, end_send, end_recv, k).wait_recv()
        for k in ks:
            lo = [ends_buf[k, 0, :, cols] for cols in columns]
            hi = [ends_buf[k, 1, :, cols] for cols in columns]
            finish(2 * k + other, lo, hi)

    @pl.loop(0, half)
    def _(t):
        finish_own(t)

    @pl.loop(0, half)
    def _(t):
        finish_theirs(t)

    for copy in (comp, row_dn, row_up, cor_dn, cor_up, edge_r, edge_l):
        copy.wait_send()
    whole(pair_tx, pair_send, ct_recv).wait_send()
    whole(end_tx, end_send, ct_recv).wait_send()
    whole(ct_rx.at[others], ct_send, ct_recv).wait_send()
    whole(ld_tx.at[others], ld_send, ct_recv).wait_send()
    whole(sol_tx.at[others], sol_send, ct_recv).wait_send()


def copy_out(parts, x_ref, out_ref, sem):
    step = x_ref.shape[0] // parts
    copies = [
        pltpu.make_async_copy(
            x_ref.at[pl.ds(n * step, step)], out_ref.at[pl.ds(n * step, step)], sem.at[n]
        )
        for n in range(parts)
    ]
    for copy in copies:
        copy.start()
    for copy in copies:
        copy.wait()


def per_device(initial_thermal_state, plate_fluid_category, corrugation_type_grid):
    nl, nr, nc = initial_thermal_state.shape
    ns, nf, nw = lax.axis_size("stack"), lax.axis_size("flow"), lax.axis_size("width")
    nch, tiles = ns // 2, nr // SUB
    total = nl * ns
    scale = STACK_SCALE * float(total * total)
    dims = (ns, nf, nw, nl, nr, nc, scale)
    f32 = jnp.float32
    packed = (tiles // PACK * SUB, LANES)
    tile_pair = pltpu.VMEM((nch, 2, SUB, nc), f32)
    dma = pltpu.SemaphoreType.DMA
    result = pl.pallas_call(
        functools.partial(kernel, dims),
        out_shape=pltpu.VMEM((nl, nr, nc), f32),
        in_specs=[
            pl.BlockSpec(memory_space=pl.ANY),
            pl.BlockSpec(memory_space=pl.ANY),
            pl.BlockSpec(memory_space=pl.ANY),
        ],
        out_specs=pl.BlockSpec(memory_space=pltpu.VMEM),
        scratch_shapes=[
            pltpu.SMEM((total,), jnp.int32),
            pltpu.VMEM((nl, nr), jnp.int32),
            pltpu.VMEM((nl, nr + 2 * SUB, nc), f32),
            pltpu.VMEM((nl, 1, nc), f32),
            pltpu.VMEM((nl, 1, nc), f32),
            pltpu.VMEM(packed, f32),
            pltpu.VMEM(packed, f32),
            pltpu.VMEM(packed, f32),
            pltpu.VMEM((nl, nr), jnp.int32),
            pltpu.VMEM((nl, nr), jnp.int32),
            pltpu.VMEM((SUB, nr), f32),
            pltpu.VMEM((SUB, nr), f32),
            pltpu.VMEM((LANES, nr), f32),
            pltpu.VMEM((nr, LANES), f32),
            pltpu.VMEM((nch, SUB, LANES), f32),
            pltpu.VMEM((7 * nl + 1, tiles, SUB, LANES), f32),
            pltpu.VMEM((6, nch, SUB, LANES), f32),
            pltpu.VMEM((tiles, SUB, nc), f32),
        ]
        + [tile_pair] * 9
        + [
            pltpu.VMEM((2 * nch, 2, SUB, LANES), f32),
            dma((LOADS + 2,)),
            dma((7,)),
            dma((7,)),
            dma,
            dma,
            dma,
            dma((nch,)),
            dma,
            dma,
            dma,
            dma((nch,)),
            dma,
            dma((nch,)),
        ]
        + [pltpu.SemaphoreType.REGULAR((2,))],
        compiler_params=pltpu.CompilerParams(
            collective_id=0,
            has_side_effects=True,
            vmem_limit_bytes=VMEM_BYTES - 4 * nl * nr * nc - (1 << 20),
        ),
        name="stack_step",
    )(plate_fluid_category, corrugation_type_grid, initial_thermal_state)
    parts = 4
    return pl.pallas_call(
        functools.partial(copy_out, parts),
        out_shape=jax.ShapeDtypeStruct((nl, nr, nc), f32),
        in_specs=[pl.BlockSpec(memory_space=pltpu.VMEM)],
        out_specs=pl.BlockSpec(memory_space=pl.ANY),
        scratch_shapes=[dma((parts,))],
        compiler_params=pltpu.CompilerParams(vmem_limit_bytes=1 << 20),
        name="copy_out",
    )(result)


def solution(mesh):
    placed = (P("stack", "flow", "width"), P(), P("stack", "flow"))
    return jax.shard_map(
        per_device,
        mesh=mesh,
        in_specs=placed,
        out_specs=P("stack", "flow", "width"),
        check_vma=False,
    )
```
